512 devices in a mesh: row: 64 (over y, z), col: 8 (over x, core).
Axes of the slice: x: 4, y: 8, z: 8, core: 2. Of those that a mesh axis runs over, the one named last changes fastest.
Arguments:
- object_field: float32 [2, 16384, 2048], P(None, 'row', 'col'), may hold values from -6 to 6
- probe_field: float32 [2, 256, 256], replicated, may hold values from -6 to 6
- amplitudes: float32 [128, 2048, 256], P('row', 'col'), may hold values from 0 to 4
- offsets: int32 [64, 8, 2, 2], P('row', 'col'), may hold values from 0 to 128, as said below
- counts: int32 [64, 8], P('row', 'col'), may hold values from 1 to 2
Outputs:
- object_out: float32 [2, 16384, 2048], P(None, 'row', 'col')
- probe_out: float32 [2, 256, 256], replicated
The draws below stay inside these ranges and needn't reach their ends.
Inputs may be any that keep to these rules, and one draw needn't show every extreme that they name: `offsets`: slots from counts[r, c] on are padding and hold no window.
All inputs are finite; a program needn't handle non-finite values.
Results may differ from the reference program's by a relative error of at most 0.0003.
Values sent between devices are 32-bit elements; how exact they have to be, the bound alone decides.
No kernel may reach another device: no remote copies, remote signals or barrier semaphores. Data moves between devices by JAX's collectives and lax.ppermute only.
A program may use at most 64 MiB of HBM per device.

```python
import jax
import jax.numpy as jnp
from jax import lax

WIN = 256
TILE = 256
HALO = 128
MOST = 2
OUTER = 2
INNER = 1
TILES_DOWN = 64
TILES_ACROSS = 8
OBJ_ROWS = 16384
OBJ_COLS = 2048


def draw_counts(key, part):
    tiles_down = OBJ_ROWS // TILE
    tiles_across = OBJ_COLS // TILE
    key_heavy = jax.random.fold_in(key, 11)
    key_light = jax.random.fold_in(key, 12)
    key_rowpick = jax.random.fold_in(key, 13)
    key_colpick = jax.random.fold_in(key, 14)
    heavy_pick = jax.random.randint(key_heavy, (tiles_down, tiles_across), 0, 4)
    lighter = jax.random.randint(key_light, (tiles_down, tiles_across), 1, MOST // 2 + 2)
    lighter = jnp.minimum(lighter, MOST)
    counted = jnp.where(heavy_pick == 0, MOST, lighter).astype(jnp.int32)
    row_spot = jax.random.randint(key_rowpick, (), 0, tiles_down)
    col_spot = jax.random.randint(key_colpick, (), 0, tiles_across)
    return counted.at[row_spot, col_spot].set(MOST).astype(jnp.int32)


def draw_offsets(key, part):
    tiles_down = OBJ_ROWS // TILE
    tiles_across = OBJ_COLS // TILE
    key_values = jax.random.fold_in(key, 21)
    key_rowpick = jax.random.fold_in(key, 22)
    key_colpick = jax.random.fold_in(key, 23)
    drawn = jax.random.randint(key_values, (tiles_down, tiles_across, MOST, 2), 0, HALO + 1)
    row_spot = jax.random.randint(key_rowpick, (), 0, tiles_down)
    col_spot = jax.random.randint(key_colpick, (), 0, tiles_across)
    other_row = (row_spot + 1) % tiles_down
    drawn = drawn.at[row_spot, col_spot, 0, :].set(HALO)
    drawn = drawn.at[other_row, col_spot, 0, :].set(0)
    return drawn.astype(jnp.int32)


def steps_of(rng, dims, cuts, low, largest):
    gain = 1.0
    for axis_at, parts in cuts:
        draws = jax.random.uniform(jax.random.fold_in(jax.random.fold_in(rng, 6), axis_at), (parts,), jnp.float32, low / len(cuts), largest / len(cuts))
        gain = gain * jnp.repeat(jnp.exp(draws), dims[axis_at] // parts).reshape((-1,) + (1,) * (len(dims) - 1 - axis_at))
    return gain


def bell_draw(own_key, dims, spread, reach, pieces=(), held_as=jnp.bfloat16):
    gain = steps_of(own_key, dims, pieces, -0.22, 0.18) if pieces else 1.0
    array = jax.random.normal(own_key, dims, jnp.float32) * spread * gain
    return jnp.minimum(jnp.maximum(array, -reach), reach).astype(held_as)


def setup_inputs(seed: int = 0) -> dict:
    streams_of = jax.random.split(jax.random.key(seed), 6)
    return {
        "object_field": bell_draw(streams_of[0], (2, OBJ_ROWS, OBJ_COLS), 1.0, 6.0, ((1, 64), (2, 8)), jnp.float32),
        "probe_field": bell_draw(streams_of[1], (2, WIN, WIN), 1.0, 6.0, (), jnp.float32),
        "amplitudes": jnp.clip(4.0 * jax.random.uniform(streams_of[2], (TILES_DOWN * MOST, TILES_ACROSS * WIN, WIN), jnp.float32) ** steps_of(streams_of[2], (TILES_DOWN * MOST, TILES_ACROSS * WIN, WIN), ((0, 64), (1, 8)), -0.2, 0.2), 0.0, 4.0),
        "offsets": draw_offsets(jax.random.fold_in(streams_of[5], 71), 0),
        "counts": draw_counts(jax.random.fold_in(streams_of[5], 71), 0),
    }


smooth_floor = 0.5
object_step = 0.5
tiny_value = 1e-06

def reference(object_field, probe_field, amplitudes, offsets, counts):
    blocks = amplitudes.reshape(TILES_DOWN, MOST, TILES_ACROSS, WIN, WIN)
    total_windows = TILES_DOWN * TILES_ACROSS * MOST
    current = object_field
    probe_now = probe_field
    for outer_step in range(OUTER):
        probe_cplx = probe_now[0] + 1j * probe_now[1]
        probe_mean = jnp.sum(probe_now * probe_now) / (WIN * WIN)
        probe_grad = jnp.zeros((2, WIN, WIN), jnp.float32)
        power_sum = jnp.zeros((), jnp.float32)
        for inner_step in range(INNER):
            padded = jnp.pad(current, ((0, 0), (0, HALO), (0, HALO)))

            def visit_window(running, flat_index):
                grad_grid, grad_probe, power_acc = running
                tile_row = flat_index // (TILES_ACROSS * MOST)
                tile_col = flat_index // MOST % TILES_ACROSS
                slot_index = flat_index % MOST
                first_row = (tile_row * TILE + offsets[tile_row, tile_col, slot_index, 0]).astype(jnp.int32)
                first_col = (tile_col * TILE + offsets[tile_row, tile_col, slot_index, 1]).astype(jnp.int32)
                zero_index = jnp.zeros((), jnp.int32)
                window_part = lax.dynamic_slice(padded, (zero_index, first_row, first_col), (2, WIN, WIN))
                measured = lax.dynamic_slice(blocks, (tile_row, slot_index, tile_col, zero_index, zero_index), (1, 1, 1, WIN, WIN))[0, 0, 0]
                live_flag = (slot_index < counts[tile_row, tile_col]).astype(jnp.float32)
                window_cplx = window_part[0] + 1j * window_part[1]
                spectrum = jnp.fft.fft2(probe_cplx * window_cplx, norm='ortho')
                magnitude = jnp.real(spectrum) ** 2 + jnp.imag(spectrum) ** 2
                ratio_term = measured / jnp.sqrt(magnitude + smooth_floor) - 1.0
                difference = jnp.fft.ifft2(spectrum * ratio_term, norm='ortho') * live_flag
                object_term = jnp.conj(probe_cplx) * difference
                probe_term = jnp.conj(window_cplx) * difference
                object_pair = jnp.stack([jnp.real(object_term), jnp.imag(object_term)])
                probe_pair = jnp.stack([jnp.real(probe_term), jnp.imag(probe_term)])
                present = lax.dynamic_slice(grad_grid, (zero_index, first_row, first_col), (2, WIN, WIN))
                grad_grid = lax.dynamic_update_slice(grad_grid, present + object_pair, (zero_index, first_row, first_col))
                power_acc = power_acc + live_flag * jnp.sum(window_part * window_part)
                return ((grad_grid, grad_probe + probe_pair, power_acc), None)
            start_state = (jnp.zeros_like(padded), jnp.zeros((2, WIN, WIN), jnp.float32), jnp.zeros((), jnp.float32))
            final_state, unused = lax.scan(visit_window, start_state, jnp.arange(total_windows, dtype=jnp.int32))
            grad_grid, grad_probe, power_acc = final_state
            current = current + object_step * grad_grid[:, :OBJ_ROWS, :OBJ_COLS] / (probe_mean + tiny_value)
            probe_grad = probe_grad + grad_probe
            power_sum = power_sum + power_acc
        moved_probe = probe_now + probe_grad / (power_sum / (WIN * WIN) + tiny_value)
        power_old = jnp.sum(probe_now * probe_now)
        power_new = jnp.sum(moved_probe * moved_probe)
        probe_now = moved_probe * jnp.sqrt(power_old / (power_new + tiny_value))
    return (current, probe_now)
```

```python
import math

import jax
import jax.numpy as jnp
from jax import lax
from jax.sharding import PartitionSpec as P

HALO = 128
OUTER = 2
NEAR = 8


smooth_floor = 0.5
object_step = 0.5
tiny_value = 1e-06


def shifted(value, axis, by):
    length = lax.axis_size(axis)
    pairs = [(i, i + by) for i in range(length) if 0 <= i + by < length]
    return lax.ppermute(value, axis, pairs)


def make_tables(length):
    indices = jnp.arange(length, dtype=jnp.int32)
    product = indices[:, None] * indices[None, :] % length
    angles = product.astype(jnp.float32) * (2.0 * math.pi / length)
    norming = 1.0 / math.sqrt(length)
    cosine_table = jnp.cos(angles) * norming
    sine_table = jnp.sin(angles) * norming
    forward = (cosine_table, -sine_table - cosine_table, cosine_table - sine_table)
    inverse = (cosine_table, sine_table - cosine_table, cosine_table + sine_table)
    return (forward, inverse)


def complex_product(real_part, imag_part, matrices, pattern):
    first_term = jnp.einsum(
        pattern, real_part + imag_part, matrices[0], precision=lax.Precision.HIGHEST
    )
    second_term = jnp.einsum(pattern, real_part, matrices[1], precision=lax.Precision.HIGHEST)
    third_term = jnp.einsum(pattern, imag_part, matrices[2], precision=lax.Precision.HIGHEST)
    return (first_term - third_term, first_term + second_term)


def transform(real_part, imag_part, matrices):
    rows_real, rows_imag = complex_product(real_part, imag_part, matrices, "bjk,kw->bjw")
    return complex_product(rows_real, rows_imag, matrices, "bkw,jk->bjw")


def window_terms(win_real, win_imag, measured, probe_real, probe_imag, forward, inverse):
    psi_real = probe_real * win_real - probe_imag * win_imag
    psi_imag = probe_real * win_imag + probe_imag * win_real
    hat_real, hat_imag = transform(psi_real, psi_imag, forward)
    ratio_term = measured / jnp.sqrt(hat_real * hat_real + hat_imag * hat_imag + smooth_floor) - 1.0
    return transform(hat_real * ratio_term, hat_imag * ratio_term, inverse)


def add_window(grid_now, terms, first_row, first_col):
    zero_index = jnp.zeros((), jnp.int32)
    present = lax.dynamic_slice(grid_now, (zero_index, first_row, first_col), terms.shape)
    return lax.dynamic_update_slice(grid_now, present + terms, (zero_index, first_row, first_col))


def device_groups(down, across, split_rows):
    far = down // NEAR
    near_groups = [
        [(y * NEAR + z) * across + c for z in range(NEAR) for c in range(across)]
        for y in range(far)
    ]
    far_groups = [
        [(y * NEAR + z) * across + c for y in range(far)]
        for z in range(NEAR)
        for c in range(across)
    ]
    return far_groups if split_rows else near_groups


def exchange(value, groups):
    return lax.all_to_all(
        value, ("row", "col"), 0, 0, tiled=True, axis_index_groups=groups
    )


def sum_everywhere(probe_grad, power_sum):
    down = lax.axis_size("row")
    across = lax.axis_size("col")
    near_groups = device_groups(down, across, False)
    far_groups = device_groups(down, across, True)
    members = len(near_groups[0])
    half = probe_grad.shape[2] // 2
    blocks = jnp.concatenate(
        [
            probe_grad[0, :, :half],
            probe_grad[0, :, half:],
            probe_grad[1, :, :half],
            probe_grad[1, :, half:],
        ]
    )
    per_member = blocks.size // members
    message = jnp.concatenate(
        [
            blocks.reshape(members, 1, per_member),
            jnp.broadcast_to(power_sum, (members, 1, half)),
        ],
        axis=2,
    )
    partial_sum = jnp.sum(exchange(message, near_groups), axis=0, keepdims=True)
    copies = jnp.broadcast_to(partial_sum, (len(far_groups[0]), 1, per_member + half))
    total = jnp.sum(exchange(copies, far_groups), axis=0)
    summed_power = total[0, per_member]
    piece = total[:, :per_member].reshape(1, per_member // half, half)
    gathered = exchange(jnp.broadcast_to(piece, (members,) + piece.shape[1:]), near_groups)
    rows = probe_grad.shape[1]
    gathered = gathered.reshape(2, 2, rows, half)
    summed_grad = jnp.concatenate([gathered[:, 0], gathered[:, 1]], axis=2)
    return summed_grad, summed_power


def shards(object_field, probe_field, amplitudes, offsets, counts):
    tile_rows = object_field.shape[1]
    tile_cols = object_field.shape[2]
    window = probe_field.shape[1]
    slot_count = amplitudes.shape[0]
    margin = HALO
    forward, inverse = make_tables(window)
    count_here = counts[0, 0]
    current = object_field
    probe_now = probe_field
    for outer_step in range(OUTER):
        probe_real = probe_now[0]
        probe_imag = probe_now[1]
        probe_mean = jnp.sum(probe_now * probe_now) / (window * window)
        lower_rows = shifted(current[:, :margin, :], "row", -1)
        taller = jnp.concatenate([current, lower_rows], axis=1)
        right_cols = shifted(taller[:, :, :margin], "col", -1)
        extended = jnp.concatenate([taller, right_cols], axis=2)
        grad_ext = jnp.zeros_like(extended)
        zero_index = jnp.zeros((), jnp.int32)
        window_list = [
            lax.dynamic_slice(
                extended,
                (zero_index, offsets[0, 0, slot_index, 0], offsets[0, 0, slot_index, 1]),
                (2, window, window),
            )
            for slot_index in range(slot_count)
        ]
        stacked = jnp.stack(window_list, axis=1)
        win_real = stacked[0]
        win_imag = stacked[1]
        diff_real, diff_imag = window_terms(
            win_real, win_imag, amplitudes, probe_real, probe_imag, forward, inverse
        )
        live_mask = (jnp.arange(slot_count, dtype=jnp.int32) < count_here).astype(jnp.float32)[
            :, None, None
        ]
        diff_real = diff_real * live_mask
        diff_imag = diff_imag * live_mask
        object_real = probe_real * diff_real + probe_imag * diff_imag
        object_imag = probe_real * diff_imag - probe_imag * diff_real
        probe_grad = jnp.stack(
            [
                jnp.sum(win_real * diff_real + win_imag * diff_imag, axis=0),
                jnp.sum(win_real * diff_imag - win_imag * diff_real, axis=0),
            ]
        )
        power_sum = jnp.sum(live_mask * (win_real * win_real + win_imag * win_imag))
        for slot_index in range(slot_count):
            terms = jnp.stack([object_real[slot_index], object_imag[slot_index]])
            grad_ext = add_window(
                grad_ext, terms, offsets[0, 0, slot_index, 0], offsets[0, 0, slot_index, 1]
            )
        rim_right = shifted(grad_ext[:, :, tile_cols:], "col", 1)
        narrowed = grad_ext[:, :, :tile_cols]
        narrowed = jnp.concatenate(
            [narrowed[:, :, :margin] + rim_right, narrowed[:, :, margin:]], axis=2
        )
        rim_lower = shifted(narrowed[:, tile_rows:, :], "row", 1)
        tile_grad = jnp.concatenate(
            [narrowed[:, :margin, :] + rim_lower, narrowed[:, margin:tile_rows, :]], axis=1
        )
        current = current + object_step * tile_grad / (probe_mean + tiny_value)
        power_old = jnp.sum(probe_now * probe_now)
        summed_grad, summed_power = sum_everywhere(probe_grad, power_sum)
        moved_probe = probe_now + summed_grad / (summed_power / (window * window) + tiny_value)
        power_new = jnp.sum(moved_probe * moved_probe)
        probe_now = moved_probe * jnp.sqrt(power_old / (power_new + tiny_value))
    return (current, probe_now)


def solution(mesh):
    return jax.shard_map(
        shards,
        mesh=mesh,
        in_specs=(
            P(None, "row", "col"),
            P(),
            P("row", "col", None),
            P("row", "col", None, None),
            P("row", "col"),
        ),
        out_specs=(P(None, "row", "col"), P()),
        check_vma=False,
    )
```

```python
import functools

import jax
import jax.numpy as jnp
import numpy as np
from jax import lax
from jax.experimental import pallas as pl
from jax.experimental.pallas import tpu as pltpu
from jax.sharding import PartitionSpec as P

HALO = 128
SUB, LANE = 8, 128
OUTER = 2
NEAR = 8

smooth_floor = 0.5
object_step = 0.5
tiny_value = 1e-06

VMEM = pl.BlockSpec(memory_space=pltpu.VMEM)
SMEM = pl.BlockSpec(memory_space=pltpu.SMEM)


def shifted(value, down_by, across_by):
    down = lax.axis_size("row")
    across = lax.axis_size("col")
    pairs = [
        (r * across + c, (r + down_by) * across + c + across_by)
        for r in range(down)
        for c in range(across)
        if 0 <= r + down_by < down and 0 <= c + across_by < across
    ]
    return lax.ppermute(value, ("row", "col"), pairs)


def device_groups(down, across):
    far = down // NEAR
    near_groups = [
        [(y * NEAR + z) * across + c for z in range(NEAR) for c in range(across)]
        for y in range(far)
    ]
    far_groups = [
        [(y * NEAR + z) * across + c for y in range(far)]
        for z in range(NEAR)
        for c in range(across)
    ]
    return near_groups, far_groups


def exchange(rows, groups):
    count, lanes = rows.shape
    paired = rows.reshape(count // 2, 2, lanes)
    moved = lax.all_to_all(
        paired, ("row", "col"), 0, 0, tiled=True, axis_index_groups=groups
    )
    return moved.reshape(count, lanes)


def make_tables(length):
    half = length // 2
    out = []
    for start in (0, 1):
        first = np.arange(half)[:, None]
        second = np.arange(start, length, 2)[None, :]
        angle = -2.0 * np.pi * ((first * second) % length) / length
        real = np.cos(angle) / np.sqrt(length)
        imag = np.sin(angle) / np.sqrt(length)
        block = np.block([[real, imag], [-imag, real]])
        for table in (block, block.T):
            high = table.astype(np.float32).astype(jnp.bfloat16)
            low = (table - high.astype(np.float64)).astype(np.float32)
            out += [high, low.astype(jnp.bfloat16)]
    return np.stack(out)


def split(value):
    high = value.astype(jnp.bfloat16)
    low = (value - high.astype(jnp.float32)).astype(jnp.bfloat16)
    return high, low


def mul(left, right):
    return jnp.dot(left, right, preferred_element_type=jnp.float32)


def mul3(left, right):
    return mul(left[0], right[0]) + (mul(left[0], right[1]) + mul(left[1], right[0]))


def edges_kernel(tile, low, right, corner):
    low[...] = tile[:, :HALO, :]
    right[...] = tile[:, :, :HALO]
    corner[...] = tile[:, :HALO, :HALO]


def order_kernel(amplitudes, pick, out, held):
    slots, size, _ = amplitudes.shape
    half = size // 2
    for slot in range(slots):
        rest = amplitudes[slot]
        total = jnp.zeros((size, size), jnp.float32)
        for _ in range(3):
            piece = rest.astype(jnp.bfloat16)
            total = total + mul(piece, pick[...])
            rest = rest - piece.astype(jnp.float32)
        for side in range(2):
            held[2 * slot + side] = total[:, side * half : (side + 1) * half]
            for part in range(2):
                out[slot, part * half : (part + 1) * half, side * half : (side + 1) * half] = held[
                    2 * slot + side, pl.ds(part, half, 2), :
                ]


def halves(row, col):
    rest = jnp.bitwise_and(row, SUB - 1)
    base = pl.multiple_of(row - rest, SUB)
    at_row = lax.broadcasted_iota(jnp.int32, (1, SUB, LANE), 1)
    at_col = lax.broadcasted_iota(jnp.int32, (1, SUB, LANE), 2)
    return rest, base, at_row, at_col


def take_window(ext, part, row, col, size):
    rest, base, at_row, at_col = halves(row, col)
    wide = ext[part, pl.ds(base, size + SUB), :]
    wide = wide.reshape(size // SUB + 1, SUB, wide.shape[1])
    turn_col = jnp.bitwise_and(LANE - col, LANE - 1)
    turn_row = jnp.bitwise_and(SUB - rest, SUB - 1)
    turned = []
    for t in range(wide.shape[2] // LANE):
        block = pltpu.roll(wide[:, :, t * LANE : (t + 1) * LANE], turn_col, 2)
        turned.append(pltpu.roll(block, turn_row, 1))
    out = []
    for t in range(len(turned) - 1):
        block = jnp.where(at_col < LANE - col, turned[t], turned[t + 1])
        block = jnp.where(at_row < SUB - rest, block[:-1], block[1:])
        out.append(block.reshape(size, LANE))
    return jnp.concatenate(out, axis=1)


def add_window(ext, part, row, col, value):
    size = value.shape[0]
    rest, base, at_row, at_col = halves(row, col)
    turn_col = jnp.bitwise_and(col, LANE - 1)
    blocks = []
    for t in range(size // LANE):
        block = value[:, t * LANE : (t + 1) * LANE].reshape(size // SUB, SUB, LANE)
        block = pltpu.roll(pltpu.roll(block, turn_col, 2), rest, 1)
        edge = jnp.zeros((1, SUB, LANE), jnp.float32)
        blocks.append(
            jnp.where(
                at_row < rest,
                jnp.concatenate([edge, block], axis=0),
                jnp.concatenate([block, edge], axis=0),
            )
        )
    none = jnp.zeros_like(blocks[0])
    blocks = [none] + blocks + [none]
    for t in range(len(blocks) - 1):
        placed = jnp.where(at_col < col, blocks[t], blocks[t + 1])
        at = (part, pl.ds(base, size + SUB), slice(t * LANE, (t + 1) * LANE))
        ext[at] = ext[at] + placed.reshape(size + SUB, LANE)


def solve_kernel(first, members, *refs):
    if first:
        (offsets, counts, tile, low, right, corner, probe, amp, tables) = refs[:9]
        message, terms, ext = refs[9:]
    else:
        (offsets, counts, tile, low, right, corner, probe, grad, power, amp, tables) = refs[:11]
        message, terms, new_probe, ext = refs[11:]
    size = tile.shape[1]
    half = size // 2
    slots = amp.shape[0]
    ext[:, :size, :size] = tile[...]
    ext[:, size : size + HALO, :size] = low[...]
    ext[:, :size, size:] = right[...]
    ext[:, size : size + HALO, size:] = corner[...]
    ext[:, size + HALO :, :] = jnp.zeros((2, SUB, size + HALO), jnp.float32)

    if first:
        p_real = probe[0]
        p_imag = probe[1]
    else:
        p_real, p_imag = moved_probe(probe, grad, power)
        new_probe[0] = p_real
        new_probe[1] = p_imag
    mean = jnp.sum(p_real * p_real + p_imag * p_imag) / (size * size)
    scale = object_step / (mean + tiny_value)

    even, even_t, odd, odd_t = (
        (tables[2 * n], tables[2 * n + 1]) for n in range(4)
    )
    pg_real = jnp.zeros((size, size), jnp.float32)
    pg_imag = jnp.zeros((size, size), jnp.float32)
    power_sum = jnp.zeros((), jnp.float32)
    for slot in range(slots):
        row = jnp.clip(offsets[slot, 0], 0, HALO)
        col = jnp.clip(offsets[slot, 1], 0, HALO)
        live = slot < counts[0]
        z_real = take_window(ext, 0, row, col, size)
        z_imag = take_window(ext, 1, row, col, size)
        psi_real = p_real * z_real - p_imag * z_imag
        psi_imag = p_real * z_imag + p_imag * z_real
        plus = jnp.concatenate(
            [psi_real[:, :half] + psi_real[:, half:], psi_imag[:, :half] + psi_imag[:, half:]], axis=1
        )
        minus = jnp.concatenate(
            [psi_real[:, :half] - psi_real[:, half:], psi_imag[:, :half] - psi_imag[:, half:]], axis=1
        )
        a_even = mul3(split(plus), even)
        a_odd = mul3(split(minus), odd)
        y_real = jnp.concatenate([a_even[:, :half], a_odd[:, :half]], axis=1)
        y_imag = jnp.concatenate([a_even[:, half:], a_odd[:, half:]], axis=1)
        plus = jnp.concatenate([y_real[:half] + y_real[half:], y_imag[:half] + y_imag[half:]], axis=0)
        minus = jnp.concatenate([y_real[:half] - y_real[half:], y_imag[:half] - y_imag[half:]], axis=0)
        sums = []
        for part, (data, table, back) in enumerate(((plus, even_t, even), (minus, odd_t, odd))):
            hat = mul3(table, split(data))
            h_real = hat[:half]
            h_imag = hat[half:]
            magnitude = h_real * h_real + h_imag * h_imag
            measured = amp[slot, part * half : (part + 1) * half, :]
            ratio = measured * lax.rsqrt(magnitude + smooth_floor) - 1.0
            scaled = jnp.concatenate([h_real * ratio, h_imag * ratio], axis=0)
            sums.append(mul3(back, split(scaled)))
        top = sums[0] + sums[1]
        bottom = sums[0] - sums[1]
        z_even = jnp.concatenate(
            [
                jnp.concatenate([top[:half, :half], top[half:, :half]], axis=1),
                jnp.concatenate([bottom[:half, :half], bottom[half:, :half]], axis=1),
            ],
            axis=0,
        )
        z_odd = jnp.concatenate(
            [
                jnp.concatenate([top[:half, half:], top[half:, half:]], axis=1),
                jnp.concatenate([bottom[:half, half:], bottom[half:, half:]], axis=1),
            ],
            axis=0,
        )
        u = mul3(split(z_even), even_t)
        v = mul3(split(z_odd), odd_t)
        plus = u + v
        minus = u - v
        d_real = jnp.concatenate([plus[:, :half], minus[:, :half]], axis=1)
        d_imag = jnp.concatenate([plus[:, half:], minus[:, half:]], axis=1)
        d_real = jnp.where(live, d_real, 0.0)
        d_imag = jnp.where(live, d_imag, 0.0)
        pg_real = pg_real + (z_real * d_real + z_imag * d_imag)
        pg_imag = pg_imag + (z_real * d_imag - z_imag * d_real)
        terms[slot, 0] = (p_real * d_real + p_imag * d_imag) * scale
        terms[slot, 1] = (p_real * d_imag - p_imag * d_real) * scale
        window_power = jnp.sum(z_real * z_real + z_imag * z_imag)
        power_sum = power_sum + jnp.where(live, window_power, 0.0)

    pieces = [pg_real[:, :half], pg_real[:, half:], pg_imag[:, :half], pg_imag[:, half:]]
    per = 4 * size // members
    for m in range(members):
        source = pieces[m * per // size]
        at = m * per % size
        message[m * (per + 2) : m * (per + 2) + per, :] = source[at : at + per, :]
        message[m * (per + 2) + per : (m + 1) * (per + 2), :] = jnp.full((2, half), power_sum)


def moved_probe(probe, grad, power):
    size = probe.shape[1]
    half = size // 2
    factor = 1.0 / (power[0:1, 0:1] / (size * size) + tiny_value)
    p_real = probe[0]
    p_imag = probe[1]
    g_real = jnp.concatenate([grad[:size, :], grad[size : 2 * size, :]], axis=1)
    g_imag = jnp.concatenate([grad[2 * size : 3 * size, :], grad[3 * size :, :]], axis=1)
    m_real = p_real + g_real * factor
    m_imag = p_imag + g_imag * factor
    old = jnp.sum(p_real * p_real + p_imag * p_imag)
    new = jnp.sum(m_real * m_real + m_imag * m_imag)
    gain = jnp.sqrt(jnp.full((1, 1), old) / (jnp.full((1, 1), new) + tiny_value))
    return m_real * gain, m_imag * gain


def probe_kernel(probe, grad, power, out):
    real, imag = moved_probe(probe, grad, power)
    out[0] = real
    out[1] = imag


def place_kernel(offsets, tile, terms, partial, rim_right, rim_low, rim_corner, ext):
    size = tile.shape[1]
    slots = terms.shape[0]
    ext[...] = jnp.zeros_like(ext)
    for slot in range(slots):
        row = jnp.clip(offsets[slot, 0], 0, HALO)
        col = jnp.clip(offsets[slot, 1], 0, HALO)
        for part in range(2):
            add_window(ext, part, row, col, terms[slot, part])
    partial[...] = tile[...] + ext[:, :size, :size]
    rim_right[...] = ext[:, :size, size:]
    rim_low[...] = ext[:, size : size + HALO, :size]
    rim_corner[...] = ext[:, size : size + HALO, size:]


def update_kernel(with_edges, partial, from_left, from_above, from_corner, out, *edges):
    size = partial.shape[1]
    out[...] = partial[...]
    out[:, :, :HALO] += from_left[...]
    out[:, :HALO, :] += from_above[...]
    out[:, :HALO, :HALO] += from_corner[...]
    if with_edges:
        edges_kernel(out, *edges)


def fold_kernel(members, copies, keep, source, out, *power):
    count = source.shape[0]
    n = count // members
    step = 4 * n
    groups = count // step
    total = source[0:step, :]
    for g in range(1, groups):
        total = total + source[g * step : (g + 1) * step, :]
    summed = total[0:n] + total[n : 2 * n] + (total[2 * n : 3 * n] + total[3 * n :])
    for c in range(copies):
        out[c * keep : (c + 1) * keep, :] = summed[:keep]
    if power:
        power[0][...] = jnp.broadcast_to(summed[n - 1 : n], power[0].shape)


def call(kernel, outs, specs, *args, scratch=()):
    return pl.pallas_call(
        kernel,
        out_shape=[jax.ShapeDtypeStruct(shape, jnp.float32) for shape in outs],
        in_specs=specs,
        out_specs=[VMEM] * len(outs),
        scratch_shapes=[pltpu.VMEM(shape, jnp.float32) for shape in scratch],
    )(*args)


def shards(object_field, probe_field, amplitudes, offsets, counts):
    _, size, _ = object_field.shape
    half = size // 2
    slots = amplitudes.shape[0]
    margin = HALO
    edge_shapes = [(2, margin, size), (2, size, margin), (2, margin, margin)]
    near_groups, far_groups = device_groups(lax.axis_size("row"), lax.axis_size("col"))
    near, far = len(near_groups[0]), len(far_groups[0])
    per = 4 * size // near
    tables = jnp.asarray(make_tables(size))
    order = np.concatenate([np.arange(0, size, 2), np.arange(1, size, 2)])
    pick = jnp.asarray(np.eye(size)[:, order].astype(jnp.bfloat16))
    spots = offsets.reshape(slots, 2)
    live = counts.reshape(1)

    current = object_field
    probe_now = probe_field
    edges = call(edges_kernel, edge_shapes, [VMEM], current)
    (amp,) = call(
        order_kernel,
        [amplitudes.shape],
        [VMEM, VMEM],
        amplitudes,
        pick,
        scratch=[(2 * slots, size, half)],
    )
    grad = power = None
    for outer_step in range(OUTER):
        low = shifted(edges[0], -1, 0)
        right = shifted(edges[1], 0, -1)
        corner = shifted(edges[2], -1, -1)
        first = outer_step == 0
        outs = [(near * (per + 2), half), (slots, 2, size, size)]
        args = [spots, live, current, low, right, corner, probe_now]
        if not first:
            outs.append((2, size, size))
            args += [grad, power]
        args += [amp, tables]
        done = call(
            functools.partial(solve_kernel, first, near),
            outs,
            [SMEM, SMEM] + [VMEM] * (len(args) - 2),
            *args,
            scratch=[(2, size + margin + SUB, size + margin)],
        )
        message, terms = done[:2]
        if not first:
            probe_now = done[2]
        arrived = exchange(message, near_groups)
        partial, rim_right, rim_low, rim_corner = call(
            place_kernel,
            [current.shape, edge_shapes[1], edge_shapes[0], edge_shapes[2]],
            [SMEM, VMEM, VMEM],
            spots,
            current,
            terms,
            scratch=[(2, size + margin + SUB, size + margin)],
        )
        from_left = shifted(rim_right, 0, 1)
        from_above = shifted(rim_low, 1, 0)
        from_corner = shifted(rim_corner, 1, 1)
        (copies,) = call(
            functools.partial(fold_kernel, near, far, per + 2),
            [(far * (per + 2), half)],
            [VMEM],
            arrived,
        )
        arrived = exchange(copies, far_groups)
        copies, power = call(
            functools.partial(fold_kernel, far, near, per),
            [(near * per, half), (8, half)],
            [VMEM],
            arrived,
        )
        grad = exchange(copies, near_groups)
        last = outer_step == OUTER - 1
        current, *edges = call(
            functools.partial(update_kernel, not last),
            [current.shape] + ([] if last else edge_shapes),
            [VMEM] * 4,
            partial,
            from_left,
            from_above,
            from_corner,
        )
    (probe_now,) = call(
        probe_kernel, [probe_field.shape], [VMEM] * 3, probe_now, grad, power
    )
    return (current, probe_now)


def solution(mesh):
    return jax.shard_map(
        shards,
        mesh=mesh,
        in_specs=(
            P(None, "row", "col"),
            P(),
            P("row", "col", None),
            P("row", "col", None, None),
            P("row", "col"),
        ),
        out_specs=(P(None, "row", "col"), P()),
        check_vma=False,
    )
```

```python
import functools

import jax
import jax.numpy as jnp
import numpy as np
from jax import lax
from jax.experimental import pallas as pl
from jax.experimental.pallas import tpu as pltpu
from jax.sharding import PartitionSpec as P


HALO = 128
SUB, LANE = 8, 128
OUTER = 2
NEAR = 8

smooth_floor = 0.5
object_step = 0.5
tiny_value = 1e-06

VMEM = pl.BlockSpec(memory_space=pltpu.VMEM)
SMEM = pl.BlockSpec(memory_space=pltpu.SMEM)


def shifted(value, down_by, across_by):
    down = lax.axis_size("row")
    across = lax.axis_size("col")
    pairs = [
        (r * across + c, (r + down_by) * across + c + across_by)
        for r in range(down)
        for c in range(across)
        if 0 <= r + down_by < down and 0 <= c + across_by < across
    ]
    return lax.ppermute(value, ("row", "col"), pairs)


def device_groups(down, across):
    far = down // NEAR
    near_groups = [
        [(y * NEAR + z) * across + x * 2 + core for z in range(NEAR) for x in range(across // 2)]
        for y in range(far)
        for core in range(2)
    ]
    far_groups = [
        [(y * NEAR + z) * across + c for y in range(far)]
        for z in range(NEAR)
        for c in range(across)
    ]
    return near_groups, far_groups


def swap_cores(value):
    across = lax.axis_size("col")
    return lax.ppermute(value, "col", [(c, c ^ 1) for c in range(across)])


def exchange(rows, groups):
    count, lanes = rows.shape
    paired = rows.reshape(count // 2, 2, lanes)
    moved = lax.all_to_all(
        paired, ("row", "col"), 0, 0, tiled=True, axis_index_groups=groups
    )
    return moved.reshape(count, lanes)


def make_tables(length):
    half = length // 2
    out = []
    for start in (0, 1):
        first = np.arange(half)[:, None]
        second = np.arange(start, length, 2)[None, :]
        angle = -2.0 * np.pi * ((first * second) % length) / length
        real = np.cos(angle) / np.sqrt(length)
        imag = np.sin(angle) / np.sqrt(length)
        block = np.block([[real, imag], [-imag, real]])
        for table in (block, block.T):
            high = table.astype(np.float32).astype(jnp.bfloat16)
            low = (table - high.astype(np.float64)).astype(np.float32)
            out += [high, low.astype(jnp.bfloat16)]
    return np.stack(out)


def split(value):
    high = value.astype(jnp.bfloat16)
    low = (value - high.astype(jnp.float32)).astype(jnp.bfloat16)
    return high, low


def mul(left, right):
    return jnp.dot(left, right, preferred_element_type=jnp.float32)


def mul3(left, right):
    return mul(left[0], right[0]) + (mul(left[0], right[1]) + mul(left[1], right[0]))


def edges_kernel(tile, low, right, corner):
    low[...] = tile[:, :HALO, :]
    right[...] = tile[:, :, :HALO]
    corner[...] = tile[:, :HALO, :HALO]


def order_kernel(amplitudes, pick, out, held):
    slots, size, _ = amplitudes.shape
    half = size // 2
    for slot in range(slots):
        rest = amplitudes[slot]
        total = jnp.zeros((size, size), jnp.float32)
        for _ in range(3):
            piece = rest.astype(jnp.bfloat16)
            total = total + mul(piece, pick[...])
            rest = rest - piece.astype(jnp.float32)
        for side in range(2):
            held[2 * slot + side] = total[:, side * half : (side + 1) * half]
            for part in range(2):
                out[slot, part * half : (part + 1) * half, side * half : (side + 1) * half] = held[
                    2 * slot + side, pl.ds(part, half, 2), :
                ]


def halves(row):
    rest = jnp.bitwise_and(row, SUB - 1)
    base = pl.multiple_of(row - rest, SUB)
    at_row = lax.broadcasted_iota(jnp.int32, (1, SUB, LANE), 1)
    at_col = lax.broadcasted_iota(jnp.int32, (1, SUB, LANE), 2)
    return rest, base, at_row, at_col


def take_window(ext, part, row, col, size):
    rest, base, at_row, at_col = halves(row)
    wide = ext[part, pl.ds(base, size + SUB), :]
    wide = wide.reshape(size // SUB + 1, SUB, wide.shape[1])
    turn_col = jnp.bitwise_and(LANE - col, LANE - 1)
    turn_row = jnp.bitwise_and(SUB - rest, SUB - 1)
    turned = []
    for t in range(wide.shape[2] // LANE):
        block = pltpu.roll(wide[:, :, t * LANE : (t + 1) * LANE], turn_col, 2)
        turned.append(pltpu.roll(block, turn_row, 1))
    out = []
    for t in range(len(turned) - 1):
        block = jnp.where(at_col < LANE - col, turned[t], turned[t + 1])
        block = jnp.where(at_row < SUB - rest, block[:-1], block[1:])
        out.append(block.reshape(size, LANE))
    return jnp.concatenate(out, axis=1)


def add_window(ext, part, row, col, value):
    size = value.shape[0]
    rest, base, at_row, at_col = halves(row)
    turn_col = jnp.bitwise_and(col, LANE - 1)
    blocks = []
    for t in range(size // LANE):
        block = value[:, t * LANE : (t + 1) * LANE].reshape(size // SUB, SUB, LANE)
        block = pltpu.roll(pltpu.roll(block, turn_col, 2), rest, 1)
        edge = jnp.zeros((1, SUB, LANE), jnp.float32)
        blocks.append(
            jnp.where(
                at_row < rest,
                jnp.concatenate([edge, block], axis=0),
                jnp.concatenate([block, edge], axis=0),
            )
        )
    none = jnp.zeros_like(blocks[0])
    blocks = [none] + blocks + [none]
    for t in range(len(blocks) - 1):
        placed = jnp.where(at_col < col, blocks[t], blocks[t + 1])
        at = (part, pl.ds(base, size + SUB), slice(t * LANE, (t + 1) * LANE))
        ext[at] = ext[at] + placed.reshape(size + SUB, LANE)


def solve_kernel(first, members, *refs):
    if first:
        (offsets, marks, tile, low, right, corner, probe, amp, tables) = refs[:9]
        keep, give, terms, ext = refs[9:]
    else:
        (offsets, marks, tile, low, right, corner, probe, mine, other, power, amp, tables) = refs[:12]
        keep, give, terms, new_probe, ext = refs[12:]
    size = tile.shape[1]
    half = size // 2
    slots = amp.shape[0]
    ext[:, :size, :size] = tile[...]
    ext[:, size : size + HALO, :size] = low[...]
    ext[:, :size, size:] = right[...]
    ext[:, size : size + HALO, size:] = corner[...]
    ext[:, size + HALO :, :] = jnp.zeros((2, SUB, size + HALO), jnp.float32)

    if first:
        p_real = probe[0]
        p_imag = probe[1]
    else:
        p_real, p_imag = moved_probe(marks, probe, mine, other, power)
        new_probe[0] = p_real
        new_probe[1] = p_imag
    mean = jnp.sum(p_real * p_real + p_imag * p_imag) / (size * size)
    scale = object_step / (mean + tiny_value)

    even, even_t, odd, odd_t = (
        (tables[2 * n], tables[2 * n + 1]) for n in range(4)
    )
    pg_real = jnp.zeros((size, size), jnp.float32)
    pg_imag = jnp.zeros((size, size), jnp.float32)
    power_sum = jnp.zeros((), jnp.float32)
    for slot in range(slots):
        row = jnp.clip(offsets[slot, 0], 0, HALO)
        col = jnp.clip(offsets[slot, 1], 0, HALO)
        live = slot < marks[0]
        z_real = take_window(ext, 0, row, col, size)
        z_imag = take_window(ext, 1, row, col, size)
        psi_real = p_real * z_real - p_imag * z_imag
        psi_imag = p_real * z_imag + p_imag * z_real
        plus = jnp.concatenate(
            [psi_real[:, :half] + psi_real[:, half:], psi_imag[:, :half] + psi_imag[:, half:]], axis=1
        )
        minus = jnp.concatenate(
            [psi_real[:, :half] - psi_real[:, half:], psi_imag[:, :half] - psi_imag[:, half:]], axis=1
        )
        a_even = mul3(split(plus), even)
        a_odd = mul3(split(minus), odd)
        y_real = jnp.concatenate([a_even[:, :half], a_odd[:, :half]], axis=1)
        y_imag = jnp.concatenate([a_even[:, half:], a_odd[:, half:]], axis=1)
        plus = jnp.concatenate([y_real[:half] + y_real[half:], y_imag[:half] + y_imag[half:]], axis=0)
        minus = jnp.concatenate([y_real[:half] - y_real[half:], y_imag[:half] - y_imag[half:]], axis=0)
        sums = []
        for part, (data, table, back) in enumerate(((plus, even_t, even), (minus, odd_t, odd))):
            hat = mul3(table, split(data))
            h_real = hat[:half]
            h_imag = hat[half:]
            magnitude = h_real * h_real + h_imag * h_imag
            measured = amp[slot, part * half : (part + 1) * half, :]
            ratio = measured * lax.rsqrt(magnitude + smooth_floor) - 1.0
            scaled = jnp.concatenate([h_real * ratio, h_imag * ratio], axis=0)
            sums.append(mul3(back, split(scaled)))
        top = sums[0] + sums[1]
        bottom = sums[0] - sums[1]
        z_even = jnp.concatenate(
            [
                jnp.concatenate([top[:half, :half], top[half:, :half]], axis=1),
                jnp.concatenate([bottom[:half, :half], bottom[half:, :half]], axis=1),
            ],
            axis=0,
        )
        z_odd = jnp.concatenate(
            [
                jnp.concatenate([top[:half, half:], top[half:, half:]], axis=1),
                jnp.concatenate([bottom[:half, half:], bottom[half:, half:]], axis=1),
            ],
            axis=0,
        )
        u = mul3(split(z_even), even_t)
        v = mul3(split(z_odd), odd_t)
        plus = u + v
        minus = u - v
        d_real = jnp.concatenate([plus[:, :half], minus[:, :half]], axis=1)
        d_imag = jnp.concatenate([plus[:, half:], minus[:, half:]], axis=1)
        d_real = jnp.where(live, d_real, 0.0)
        d_imag = jnp.where(live, d_imag, 0.0)
        pg_real = pg_real + (z_real * d_real + z_imag * d_imag)
        pg_imag = pg_imag + (z_real * d_imag - z_imag * d_real)
        terms[slot, 0] = (p_real * d_real + p_imag * d_imag) * scale
        terms[slot, 1] = (p_real * d_imag - p_imag * d_real) * scale
        window_power = jnp.sum(z_real * z_real + z_imag * z_imag)
        power_sum = power_sum + jnp.where(live, window_power, 0.0)

    second = marks[1] == 1
    per = 2 * size // members
    for half_at in range(2):
        columns = slice(half_at * half, (half_at + 1) * half)
        kept = jnp.where(second, pg_imag[:, columns], pg_real[:, columns])
        given = jnp.where(second, pg_real[:, columns], pg_imag[:, columns])
        for m in range(members // 2):
            at = (half_at * members // 2 + m) * (per + 2)
            for ref, value in ((keep, kept), (give, given)):
                ref[at : at + per, :] = value[m * per : (m + 1) * per, :]
                ref[at + per : at + per + 2, :] = jnp.full((2, half), power_sum)


def moved_probe(marks, probe, mine, other, power):
    size = probe.shape[1]
    second = marks[1] == 1
    factor = 1.0 / (power[0:1, 0:1] / (size * size) + tiny_value)
    p_real = probe[0]
    p_imag = probe[1]
    one = jnp.concatenate([mine[:size, :], mine[size:, :]], axis=1)
    two = jnp.concatenate([other[:size, :], other[size:, :]], axis=1)
    m_real = p_real + jnp.where(second, two, one) * factor
    m_imag = p_imag + jnp.where(second, one, two) * factor
    old = jnp.sum(p_real * p_real + p_imag * p_imag)
    new = jnp.sum(m_real * m_real + m_imag * m_imag)
    gain = jnp.sqrt(jnp.full((1, 1), old) / (jnp.full((1, 1), new) + tiny_value))
    return m_real * gain, m_imag * gain


def probe_kernel(marks, probe, mine, other, power, out):
    real, imag = moved_probe(marks, probe, mine, other, power)
    out[0] = real
    out[1] = imag


def place_kernel(offsets, tile, terms, partial, rim_right, rim_low, rim_corner, ext):
    size = tile.shape[1]
    slots = terms.shape[0]
    ext[...] = jnp.zeros_like(ext)
    for slot in range(slots):
        row = jnp.clip(offsets[slot, 0], 0, HALO)
        col = jnp.clip(offsets[slot, 1], 0, HALO)
        for part in range(2):
            add_window(ext, part, row, col, terms[slot, part])
    partial[...] = tile[...] + ext[:, :size, :size]
    rim_right[...] = ext[:, :size, size:]
    rim_low[...] = ext[:, size : size + HALO, :size]
    rim_corner[...] = ext[:, size : size + HALO, size:]


def update_kernel(with_edges, partial, from_left, from_above, from_corner, out, *edges):
    out[...] = partial[...]
    out[:, :, :HALO] += from_left[...]
    out[:, :HALO, :] += from_above[...]
    out[:, :HALO, :HALO] += from_corner[...]
    if with_edges:
        edges_kernel(out, *edges)


def fold_kernel(members, copies, keep, source, out, *power):
    count = source.shape[0]
    n = count // members
    step = 4 * n
    groups = count // step
    total = source[0:step, :]
    for g in range(1, groups):
        total = total + source[g * step : (g + 1) * step, :]
    summed = total[0:n] + total[n : 2 * n] + (total[2 * n : 3 * n] + total[3 * n :])
    for c in range(copies):
        out[c * keep : (c + 1) * keep, :] = summed[:keep]
    if power:
        power[0][...] = jnp.broadcast_to(summed[n - 1 : n], power[0].shape)


def call(kernel, outs, specs, *args, scratch=(), grant=6):
    return pl.pallas_call(
        kernel,
        out_shape=[jax.ShapeDtypeStruct(shape, jnp.float32) for shape in outs],
        in_specs=specs,
        out_specs=[VMEM] * len(outs),
        scratch_shapes=[pltpu.VMEM(shape, jnp.float32) for shape in scratch],
        compiler_params=pltpu.CompilerParams(vmem_limit_bytes=grant << 20),
    )(*args)


def halo(edges):
    return shifted(edges[0], -1, 0), shifted(edges[1], 0, -1), shifted(edges[2], -1, -1)


def shards(object_field, probe_field, amplitudes, offsets, counts):
    _, size, _ = object_field.shape
    half = size // 2
    slots = amplitudes.shape[0]
    margin = HALO
    edge_shapes = [(2, margin, size), (2, size, margin), (2, margin, margin)]
    near_groups, far_groups = device_groups(lax.axis_size("row"), lax.axis_size("col"))
    near, far = len(near_groups[0]), len(far_groups[0])
    per = 2 * size // near
    held = near * (per + 2)
    tables = jnp.asarray(make_tables(size))
    order = np.concatenate([np.arange(0, size, 2), np.arange(1, size, 2)])
    pick = jnp.asarray(np.eye(size)[:, order].astype(jnp.bfloat16))
    spots = offsets.reshape(slots, 2)
    core = jnp.bitwise_and(lax.axis_index("col"), 1).astype(jnp.int32)
    marks = jnp.concatenate([counts.reshape(1), core.reshape(1)])

    current = object_field
    probe_now = probe_field
    edges = call(edges_kernel, edge_shapes, [VMEM], current)
    (amp,) = call(
        order_kernel,
        [amplitudes.shape],
        [VMEM, VMEM],
        amplitudes,
        pick,
        scratch=[(2 * slots, size, half)],
    )
    low, right, corner = halo(edges)
    mine = other = power = None
    for outer_step in range(OUTER):
        first = outer_step == 0
        outs = [(held, half), (held, half), (slots, 2, size, size)]
        args = [spots, marks, current, low, right, corner, probe_now]
        if not first:
            outs.append((2, size, size))
            args += [mine, other, power]
        args += [amp, tables]
        done = call(
            functools.partial(solve_kernel, first, near),
            outs,
            [SMEM, SMEM] + [VMEM] * (len(args) - 2),
            *args,
            scratch=[(2, size + margin + SUB, size + margin)],
            grant=14,
        )
        keep, give, terms = done[:3]
        if not first:
            probe_now = done[3]
        given = swap_cores(give)
        partial, rim_right, rim_low, rim_corner = call(
            place_kernel,
            [current.shape, edge_shapes[1], edge_shapes[0], edge_shapes[2]],
            [SMEM, VMEM, VMEM],
            spots,
            current,
            terms,
            scratch=[(2, size + margin + SUB, size + margin)],
            grant=6,
        )
        arrived = exchange(keep + given, near_groups)
        from_left = shifted(rim_right, 0, 1)
        from_above = shifted(rim_low, 1, 0)
        from_corner = shifted(rim_corner, 1, 1)
        (copies,) = call(
            functools.partial(fold_kernel, near, far, per + 2),
            [(far * (per + 2), half)],
            [VMEM],
            arrived,
        )
        arrived = exchange(copies, far_groups)
        copies, power = call(
            functools.partial(fold_kernel, far, near, per),
            [(near * per, half), (8, half)],
            [VMEM],
            arrived,
        )
        mine = exchange(copies, near_groups)
        other = swap_cores(mine)
        last = outer_step == OUTER - 1
        current, *edges = call(
            functools.partial(update_kernel, not last),
            [current.shape] + ([] if last else edge_shapes),
            [VMEM] * 4,
            partial,
            from_left,
            from_above,
            from_corner,
        )
        if not last:
            low, right, corner = halo(edges)
    (probe_now,) = call(
        probe_kernel,
        [probe_field.shape],
        [SMEM] + [VMEM] * 4,
        marks,
        probe_now,
        mine,
        other,
        power,
    )
    return (current, probe_now)


def solution(mesh):
    return jax.shard_map(
        shards,
        mesh=mesh,
        in_specs=(
            P(None, "row", "col"),
            P(),
            P("row", "col", None),
            P("row", "col", None, None),
            P("row", "col"),
        ),
        out_specs=(P(None, "row", "col"), P()),
        check_vma=False,
    )
```

```python
import functools

import jax
import jax.numpy as jnp
import numpy as np
from jax import lax
from jax.experimental import pallas as pl
from jax.experimental.pallas import tpu as pltpu
from jax.sharding import PartitionSpec as P


HALO = 128
SUB, LANE = 8, 128
OUTER = 2
NEAR = 8

smooth_floor = 0.5
object_step = 0.5
tiny_value = 1e-06

VMEM = pl.BlockSpec(memory_space=pltpu.VMEM)
SMEM = pl.BlockSpec(memory_space=pltpu.SMEM)


def shifted(value, down_by, across_by):
    down = lax.axis_size("row")
    across = lax.axis_size("col")
    pairs = [
        (r * across + c, (r + down_by) * across + c + across_by)
        for r in range(down)
        for c in range(across)
        if 0 <= r + down_by < down and 0 <= c + across_by < across
    ]
    return lax.ppermute(value, ("row", "col"), pairs)


def device_groups(down, across):
    far = down // NEAR
    near_groups = [
        [(y * NEAR + z) * across + x * 2 + core for z in range(NEAR) for x in range(across // 2)]
        for y in range(far)
        for core in range(2)
    ]
    far_groups = [
        [(y * NEAR + z) * across + c for y in range(far)]
        for z in range(NEAR)
        for c in range(across)
    ]
    return near_groups, far_groups


def swap_cores(value):
    across = lax.axis_size("col")
    return lax.ppermute(value, "col", [(c, c ^ 1) for c in range(across)])


def exchange(rows, groups):
    count, lanes = rows.shape
    paired = rows.reshape(count // 2, 2, lanes)
    moved = lax.all_to_all(
        paired, ("row", "col"), 0, 0, tiled=True, axis_index_groups=groups
    )
    return moved.reshape(count, lanes)


def make_tables(length):
    half = length // 2
    out = []
    for start in (0, 1):
        first = np.arange(half)[:, None]
        second = np.arange(start, length, 2)[None, :]
        angle = -2.0 * np.pi * ((first * second) % length) / length
        real = np.cos(angle) / np.sqrt(length)
        imag = np.sin(angle) / np.sqrt(length)
        block = np.block([[real, imag], [-imag, real]])
        for table in (block, block.T):
            high = table.astype(np.float32).astype(jnp.bfloat16)
            low = (table - high.astype(np.float64)).astype(np.float32)
            out += [high, low.astype(jnp.bfloat16)]
    return np.stack(out)


def split(value):
    high = value.astype(jnp.bfloat16)
    low = (value - high.astype(jnp.float32)).astype(jnp.bfloat16)
    return high, low


def mul(left, right):
    return jnp.dot(left, right, preferred_element_type=jnp.float32)


def mul3(left, right):
    return mul(left[0], right[0]) + (mul(left[0], right[1]) + mul(left[1], right[0]))


def edges_kernel(tile, low, right, corner):
    low[...] = tile[:, :HALO, :]
    right[...] = tile[:, :, :HALO]
    corner[...] = tile[:, :HALO, :HALO]


def order_kernel(amplitudes, pick, probe, out, probe_out, held):
    slots, size, _ = amplitudes.shape
    half = size // 2
    probe_out[...] = probe[...]
    for slot in range(slots):
        rest = amplitudes[slot]
        total = jnp.zeros((size, size), jnp.float32)
        for _ in range(3):
            piece = rest.astype(jnp.bfloat16)
            total = total + mul(piece, pick[...])
            rest = rest - piece.astype(jnp.float32)
        for side in range(2):
            held[2 * slot + side] = total[:, side * half : (side + 1) * half]
            for part in range(2):
                out[slot, part * half : (part + 1) * half, side * half : (side + 1) * half] = held[
                    2 * slot + side, pl.ds(part, half, 2), :
                ]


def halves(row):
    rest = jnp.bitwise_and(row, SUB - 1)
    base = pl.multiple_of(row - rest, SUB)
    at_row = lax.broadcasted_iota(jnp.int32, (1, SUB, LANE), 1)
    at_col = lax.broadcasted_iota(jnp.int32, (1, SUB, LANE), 2)
    return rest, base, at_row, at_col


def take_window(ext, part, row, col, size):
    rest, base, at_row, at_col = halves(row)
    wide = ext[part, pl.ds(base, size + SUB), :]
    wide = wide.reshape(size // SUB + 1, SUB, wide.shape[1])
    turn_col = jnp.bitwise_and(LANE - col, LANE - 1)
    turn_row = jnp.bitwise_and(SUB - rest, SUB - 1)
    turned = []
    for t in range(wide.shape[2] // LANE):
        block = pltpu.roll(wide[:, :, t * LANE : (t + 1) * LANE], turn_col, 2)
        turned.append(pltpu.roll(block, turn_row, 1))
    out = []
    for t in range(len(turned) - 1):
        block = jnp.where(at_col < LANE - col, turned[t], turned[t + 1])
        block = jnp.where(at_row < SUB - rest, block[:-1], block[1:])
        out.append(block.reshape(size, LANE))
    return jnp.concatenate(out, axis=1)


def add_window(ext, part, row, col, value):
    size = value.shape[0]
    rest, base, at_row, at_col = halves(row)
    turn_col = jnp.bitwise_and(col, LANE - 1)
    blocks = []
    for t in range(size // LANE):
        block = value[:, t * LANE : (t + 1) * LANE].reshape(size // SUB, SUB, LANE)
        block = pltpu.roll(pltpu.roll(block, turn_col, 2), rest, 1)
        edge = jnp.zeros((1, SUB, LANE), jnp.float32)
        blocks.append(
            jnp.where(
                at_row < rest,
                jnp.concatenate([edge, block], axis=0),
                jnp.concatenate([block, edge], axis=0),
            )
        )
    none = jnp.zeros_like(blocks[0])
    blocks = [none] + blocks + [none]
    for t in range(len(blocks) - 1):
        placed = jnp.where(at_col < col, blocks[t], blocks[t + 1])
        at = (part, pl.ds(base, size + SUB), slice(t * LANE, (t + 1) * LANE))
        ext[at] = ext[at] + placed.reshape(size + SUB, LANE)


def solve_kernel(first, members, *refs):
    if first:
        (offsets, marks, tile, low, right, corner, probe, amp, tables) = refs[:9]
        keep, give, terms, ext = refs[9:]
    else:
        (offsets, marks, tile, low, right, corner, probe, mine, other, power, amp, tables) = refs[:12]
        keep, give, terms, new_probe, ext = refs[12:]
    size = tile.shape[1]
    half = size // 2
    slots = amp.shape[0]
    ext[:, :size, :size] = tile[...]
    ext[:, size : size + HALO, :size] = low[...]
    ext[:, :size, size:] = right[...]
    ext[:, size : size + HALO, size:] = corner[...]
    ext[:, size + HALO :, :] = jnp.zeros((2, SUB, size + HALO), jnp.float32)

    if first:
        p_real = probe[0]
        p_imag = probe[1]
    else:
        p_real, p_imag = moved_probe(marks, probe, mine, other, power)
        new_probe[0] = p_real
        new_probe[1] = p_imag
    mean = jnp.sum(p_real * p_real + p_imag * p_imag) / (size * size)
    scale = object_step / (mean + tiny_value)

    even, even_t, odd, odd_t = (
        (tables[2 * n], tables[2 * n + 1]) for n in range(4)
    )
    pg_real = jnp.zeros((size, size), jnp.float32)
    pg_imag = jnp.zeros((size, size), jnp.float32)
    power_sum = jnp.zeros((), jnp.float32)
    for slot in range(slots):
        row = jnp.clip(offsets[slot, 0], 0, HALO)
        col = jnp.clip(offsets[slot, 1], 0, HALO)
        live = slot < marks[0]
        z_real = take_window(ext, 0, row, col, size)
        z_imag = take_window(ext, 1, row, col, size)
        psi_real = p_real * z_real - p_imag * z_imag
        psi_imag = p_real * z_imag + p_imag * z_real
        plus = jnp.concatenate(
            [psi_real[:, :half] + psi_real[:, half:], psi_imag[:, :half] + psi_imag[:, half:]], axis=1
        )
        minus = jnp.concatenate(
            [psi_real[:, :half] - psi_real[:, half:], psi_imag[:, :half] - psi_imag[:, half:]], axis=1
        )
        a_even = mul3(split(plus), even)
        a_odd = mul3(split(minus), odd)
        y_real = jnp.concatenate([a_even[:, :half], a_odd[:, :half]], axis=1)
        y_imag = jnp.concatenate([a_even[:, half:], a_odd[:, half:]], axis=1)
        plus = jnp.concatenate([y_real[:half] + y_real[half:], y_imag[:half] + y_imag[half:]], axis=0)
        minus = jnp.concatenate([y_real[:half] - y_real[half:], y_imag[:half] - y_imag[half:]], axis=0)
        sums = []
        for part, (data, table, back) in enumerate(((plus, even_t, even), (minus, odd_t, odd))):
            hat = mul3(table, split(data))
            h_real = hat[:half]
            h_imag = hat[half:]
            magnitude = h_real * h_real + h_imag * h_imag
            measured = amp[slot, part * half : (part + 1) * half, :]
            ratio = measured * lax.rsqrt(magnitude + smooth_floor) - 1.0
            scaled = jnp.concatenate([h_real * ratio, h_imag * ratio], axis=0)
            sums.append(mul3(back, split(scaled)))
        top = sums[0] + sums[1]
        bottom = sums[0] - sums[1]
        z_even = jnp.concatenate(
            [
                jnp.concatenate([top[:half, :half], top[half:, :half]], axis=1),
                jnp.concatenate([bottom[:half, :half], bottom[half:, :half]], axis=1),
            ],
            axis=0,
        )
        z_odd = jnp.concatenate(
            [
                jnp.concatenate([top[:half, half:], top[half:, half:]], axis=1),
                jnp.concatenate([bottom[:half, half:], bottom[half:, half:]], axis=1),
            ],
            axis=0,
        )
        u = mul3(split(z_even), even_t)
        v = mul3(split(z_odd), odd_t)
        plus = u + v
        minus = u - v
        d_real = jnp.concatenate([plus[:, :half], minus[:, :half]], axis=1)
        d_imag = jnp.concatenate([plus[:, half:], minus[:, half:]], axis=1)
        d_real = jnp.where(live, d_real, 0.0)
        d_imag = jnp.where(live, d_imag, 0.0)
        pg_real = pg_real + (z_real * d_real + z_imag * d_imag)
        pg_imag = pg_imag + (z_real * d_imag - z_imag * d_real)
        terms[slot, 0] = (p_real * d_real + p_imag * d_imag) * scale
        terms[slot, 1] = (p_real * d_imag - p_imag * d_real) * scale
        window_power = jnp.sum(z_real * z_real + z_imag * z_imag)
        power_sum = power_sum + jnp.where(live, window_power, 0.0)

    second = marks[1] == 1
    per = 2 * size // members
    for half_at in range(2):
        columns = slice(half_at * half, (half_at + 1) * half)
        kept = jnp.where(second, pg_imag[:, columns], pg_real[:, columns])
        given = jnp.where(second, pg_real[:, columns], pg_imag[:, columns])
        for m in range(members // 2):
            at = (half_at * members // 2 + m) * (per + 2)
            for ref, value in ((keep, kept), (give, given)):
                ref[at : at + per, :] = value[m * per : (m + 1) * per, :]
                ref[at + per : at + per + 2, :] = jnp.full((2, half), power_sum)


def moved_probe(marks, probe, mine, other, power):
    size = probe.shape[1]
    second = marks[1] == 1
    factor = 1.0 / (power[0:1, 0:1] / (size * size) + tiny_value)
    p_real = probe[0]
    p_imag = probe[1]
    one = jnp.concatenate([mine[:size, :], mine[size:, :]], axis=1)
    two = jnp.concatenate([other[:size, :], other[size:, :]], axis=1)
    m_real = p_real + jnp.where(second, two, one) * factor
    m_imag = p_imag + jnp.where(second, one, two) * factor
    old = jnp.sum(p_real * p_real + p_imag * p_imag)
    new = jnp.sum(m_real * m_real + m_imag * m_imag)
    gain = jnp.sqrt(jnp.full((1, 1), old) / (jnp.full((1, 1), new) + tiny_value))
    return m_real * gain, m_imag * gain


def probe_kernel(marks, probe, mine, other, power, out):
    real, imag = moved_probe(marks, probe, mine, other, power)
    out[0] = real
    out[1] = imag


def place_kernel(offsets, tile, terms, partial, rim_right, rim_low, rim_corner, ext):
    size = tile.shape[1]
    slots = terms.shape[0]
    ext[...] = jnp.zeros_like(ext)
    for slot in range(slots):
        row = jnp.clip(offsets[slot, 0], 0, HALO)
        col = jnp.clip(offsets[slot, 1], 0, HALO)
        for part in range(2):
            add_window(ext, part, row, col, terms[slot, part])
    partial[...] = tile[...] + ext[:, :size, :size]
    rim_right[...] = ext[:, :size, size:]
    rim_low[...] = ext[:, size : size + HALO, :size]
    rim_corner[...] = ext[:, size : size + HALO, size:]


def update_kernel(with_edges, partial, from_left, from_above, from_corner, out, *edges):
    out[...] = partial[...]
    out[:, :, :HALO] += from_left[...]
    out[:, :HALO, :] += from_above[...]
    out[:, :HALO, :HALO] += from_corner[...]
    if with_edges:
        edges_kernel(out, *edges)


def fold_kernel(members, copies, keep, source, out, *power):
    count = source.shape[0]
    n = count // members
    step = 4 * n
    groups = count // step
    total = source[0:step, :]
    for g in range(1, groups):
        total = total + source[g * step : (g + 1) * step, :]
    summed = total[0:n] + total[n : 2 * n] + (total[2 * n : 3 * n] + total[3 * n :])
    for c in range(copies):
        out[c * keep : (c + 1) * keep, :] = summed[:keep]
    if power:
        power[0][...] = jnp.broadcast_to(summed[n - 1 : n], power[0].shape)


def call(kernel, outs, specs, *args, scratch=(), grant=2):
    return pl.pallas_call(
        kernel,
        out_shape=[jax.ShapeDtypeStruct(shape, jnp.float32) for shape in outs],
        in_specs=specs,
        out_specs=[VMEM] * len(outs),
        scratch_shapes=[pltpu.VMEM(shape, jnp.float32) for shape in scratch],
        compiler_params=pltpu.CompilerParams(vmem_limit_bytes=grant << 20),
    )(*args)


def halo(edges):
    return shifted(edges[0], -1, 0), shifted(edges[1], 0, -1), shifted(edges[2], -1, -1)


def shards(object_field, probe_field, amplitudes, offsets, counts):
    _, size, _ = object_field.shape
    half = size // 2
    slots = amplitudes.shape[0]
    margin = HALO
    edge_shapes = [(2, margin, size), (2, size, margin), (2, margin, margin)]
    near_groups, far_groups = device_groups(lax.axis_size("row"), lax.axis_size("col"))
    near, far = len(near_groups[0]), len(far_groups[0])
    per = 2 * size // near
    held = near * (per + 2)
    tables = jnp.asarray(make_tables(size))
    order = np.concatenate([np.arange(0, size, 2), np.arange(1, size, 2)])
    pick = jnp.asarray(np.eye(size)[:, order].astype(jnp.bfloat16))
    spots = offsets.reshape(slots, 2)
    core = jnp.bitwise_and(lax.axis_index("col"), 1).astype(jnp.int32)
    marks = jnp.concatenate([counts.reshape(1), core.reshape(1)])

    current = object_field
    edges = call(edges_kernel, edge_shapes, [VMEM], current)
    amp, probe_now = call(
        order_kernel,
        [amplitudes.shape, probe_field.shape],
        [VMEM] * 3,
        amplitudes,
        pick,
        probe_field,
        scratch=[(2 * slots, size, half)],
    )
    low, right, corner = halo(edges)
    mine = other = power = None
    for outer_step in range(OUTER):
        first = outer_step == 0
        outs = [(held, half), (held, half), (slots, 2, size, size)]
        args = [spots, marks, current, low, right, corner, probe_now]
        if not first:
            outs.append((2, size, size))
            args += [mine, other, power]
        args += [amp, tables]
        done = call(
            functools.partial(solve_kernel, first, near),
            outs,
            [SMEM, SMEM] + [VMEM] * (len(args) - 2),
            *args,
            scratch=[(2, size + margin + SUB, size + margin)],
            grant=8,
        )
        keep, give, terms = done[:3]
        if not first:
            probe_now = done[3]
        given = swap_cores(give)
        partial, rim_right, rim_low, rim_corner = call(
            place_kernel,
            [current.shape, edge_shapes[1], edge_shapes[0], edge_shapes[2]],
            [SMEM, VMEM, VMEM],
            spots,
            current,
            terms,
            scratch=[(2, size + margin + SUB, size + margin)],
            grant=3,
        )
        from_left = shifted(rim_right, 0, 1)
        from_above = shifted(rim_low, 1, 0)
        from_corner = shifted(rim_corner, 1, 1)
        arrived = exchange(keep + given, near_groups)
        (copies,) = call(
            functools.partial(fold_kernel, near, far, per + 2),
            [(far * (per + 2), half)],
            [VMEM],
            arrived,
        )
        arrived = exchange(copies, far_groups)
        copies, power = call(
            functools.partial(fold_kernel, far, near, per),
            [(near * per, half), (8, half)],
            [VMEM],
            arrived,
        )
        mine = exchange(copies, near_groups)
        other = swap_cores(mine)
        last = outer_step == OUTER - 1
        current, *edges = call(
            functools.partial(update_kernel, not last),
            [current.shape] + ([] if last else edge_shapes),
            [VMEM] * 4,
            partial,
            from_left,
            from_above,
            from_corner,
        )
        if not last:
            low, right, corner = halo(edges)
    (probe_now,) = call(
        probe_kernel,
        [probe_field.shape],
        [SMEM] + [VMEM] * 4,
        marks,
        probe_now,
        mine,
        other,
        power,
    )
    return (current, probe_now)


def solution(mesh):
    return jax.shard_map(
        shards,
        mesh=mesh,
        in_specs=(
            P(None, "row", "col"),
            P(),
            P("row", "col", None),
            P("row", "col", None, None),
            P("row", "col"),
        ),
        out_specs=(P(None, "row", "col"), P()),
        check_vma=False,
    )
```

```python
import functools

import jax
import jax.numpy as jnp
import numpy as np
from jax import lax
from jax.experimental import pallas as pl
from jax.experimental.pallas import tpu as pltpu
from jax.sharding import PartitionSpec as P


HALO = 128
SUB, LANE = 8, 128
OUTER = 2
NEAR = 8

smooth_floor = 0.5
object_step = 0.5
tiny_value = 1e-06

VMEM = pl.BlockSpec(memory_space=pltpu.VMEM)
SMEM = pl.BlockSpec(memory_space=pltpu.SMEM)


def shifted(value, down_by, across_by):
    down = lax.axis_size("row")
    across = lax.axis_size("col")
    pairs = [
        (r * across + c, (r + down_by) * across + c + across_by)
        for r in range(down)
        for c in range(across)
        if 0 <= r + down_by < down and 0 <= c + across_by < across
    ]
    return lax.ppermute(value, ("row", "col"), pairs)


def device_groups(down, across):
    far = down // NEAR
    wide_groups = [
        [(y * NEAR + z) * across + x * 2 + core for y in range(far) for x in range(across // 2)]
        for z in range(NEAR)
        for core in range(2)
    ]
    line_groups = [
        [(y * NEAR + z) * across + c for z in range(NEAR)]
        for y in range(far)
        for c in range(across)
    ]
    return wide_groups, line_groups


def swap_cores(value):
    across = lax.axis_size("col")
    return lax.ppermute(value, "col", [(c, c ^ 1) for c in range(across)])


def exchange(rows, groups):
    count, lanes = rows.shape
    paired = rows.reshape(count // 2, 2, lanes)
    moved = lax.all_to_all(
        paired, ("row", "col"), 0, 0, tiled=True, axis_index_groups=groups
    )
    return moved.reshape(count, lanes)


def make_tables(length):
    half = length // 2
    out = []
    for start in (0, 1):
        first = np.arange(half)[:, None]
        second = np.arange(start, length, 2)[None, :]
        angle = -2.0 * np.pi * ((first * second) % length) / length
        real = np.cos(angle) / np.sqrt(length)
        imag = np.sin(angle) / np.sqrt(length)
        block = np.block([[real, imag], [-imag, real]])
        for table in (block, block.T):
            high = table.astype(np.float32).astype(jnp.bfloat16)
            low = (table - high.astype(np.float64)).astype(np.float32)
            out += [high, low.astype(jnp.bfloat16)]
    return np.stack(out)


def split(value):
    high = value.astype(jnp.bfloat16)
    low = (value - high.astype(jnp.float32)).astype(jnp.bfloat16)
    return high, low


def mul(left, right):
    return jnp.dot(left, right, preferred_element_type=jnp.float32)


def mul3(left, right):
    return mul(left[0], right[0]) + (mul(left[0], right[1]) + mul(left[1], right[0]))


def edges_kernel(tile, low, right, corner):
    low[...] = tile[:, :HALO, :]
    right[...] = tile[:, :, :HALO]
    corner[...] = tile[:, :HALO, :HALO]


def order_kernel(amplitudes, pick, probe, out, probe_out, held):
    slots, size, _ = amplitudes.shape
    half = size // 2
    probe_out[...] = probe[...]
    for slot in range(slots):
        rest = amplitudes[slot]
        total = jnp.zeros((size, size), jnp.float32)
        for _ in range(3):
            piece = rest.astype(jnp.bfloat16)
            total = total + mul(piece, pick[...])
            rest = rest - piece.astype(jnp.float32)
        for side in range(2):
            held[2 * slot + side] = total[:, side * half : (side + 1) * half]
            for part in range(2):
                out[slot, part * half : (part + 1) * half, side * half : (side + 1) * half] = held[
                    2 * slot + side, pl.ds(part, half, 2), :
                ]


def halves(row):
    rest = jnp.bitwise_and(row, SUB - 1)
    base = pl.multiple_of(row - rest, SUB)
    at_row = lax.broadcasted_iota(jnp.int32, (1, SUB, LANE), 1)
    at_col = lax.broadcasted_iota(jnp.int32, (1, SUB, LANE), 2)
    return rest, base, at_row, at_col


def take_window(ext, part, row, col, size):
    rest, base, at_row, at_col = halves(row)
    wide = ext[part, pl.ds(base, size + SUB), :]
    wide = wide.reshape(size // SUB + 1, SUB, wide.shape[1])
    turn_col = jnp.bitwise_and(LANE - col, LANE - 1)
    turn_row = jnp.bitwise_and(SUB - rest, SUB - 1)
    turned = []
    for t in range(wide.shape[2] // LANE):
        block = pltpu.roll(wide[:, :, t * LANE : (t + 1) * LANE], turn_col, 2)
        turned.append(pltpu.roll(block, turn_row, 1))
    out = []
    for t in range(len(turned) - 1):
        block = jnp.where(at_col < LANE - col, turned[t], turned[t + 1])
        block = jnp.where(at_row < SUB - rest, block[:-1], block[1:])
        out.append(block.reshape(size, LANE))
    return jnp.concatenate(out, axis=1)


def add_window(ext, part, row, col, value):
    size = value.shape[0]
    rest, base, at_row, at_col = halves(row)
    turn_col = jnp.bitwise_and(col, LANE - 1)
    blocks = []
    for t in range(size // LANE):
        block = value[:, t * LANE : (t + 1) * LANE].reshape(size // SUB, SUB, LANE)
        block = pltpu.roll(pltpu.roll(block, turn_col, 2), rest, 1)
        edge = jnp.zeros((1, SUB, LANE), jnp.float32)
        blocks.append(
            jnp.where(
                at_row < rest,
                jnp.concatenate([edge, block], axis=0),
                jnp.concatenate([block, edge], axis=0),
            )
        )
    none = jnp.zeros_like(blocks[0])
    blocks = [none] + blocks + [none]
    for t in range(len(blocks) - 1):
        placed = jnp.where(at_col < col, blocks[t], blocks[t + 1])
        at = (part, pl.ds(base, size + SUB), slice(t * LANE, (t + 1) * LANE))
        ext[at] = ext[at] + placed.reshape(size + SUB, LANE)


def solve_kernel(first, members, *refs):
    if first:
        (marks, tile, low, right, corner, probe, amp, tables) = refs[:8]
        keep, give, terms, ext = refs[8:]
    else:
        (marks, tile, low, right, corner, probe, mine, other, power, amp, tables) = refs[:11]
        keep, give, terms, new_probe, ext = refs[11:]
    size = tile.shape[1]
    half = size // 2
    slots = amp.shape[0]
    ext[:, :size, :size] = tile[...]
    ext[:, size : size + HALO, :size] = low[...]
    ext[:, :size, size:] = right[...]
    ext[:, size : size + HALO, size:] = corner[...]
    ext[:, size + HALO :, :] = jnp.zeros((2, SUB, size + HALO), jnp.float32)

    if first:
        p_real = probe[0]
        p_imag = probe[1]
    else:
        p_real, p_imag = moved_probe(marks, probe, mine, other, power)
        new_probe[0] = p_real
        new_probe[1] = p_imag
    mean = jnp.sum(p_real * p_real + p_imag * p_imag) / (size * size)
    scale = object_step / (mean + tiny_value)

    even, even_t, odd, odd_t = (
        (tables[2 * n], tables[2 * n + 1]) for n in range(4)
    )
    pg_real = jnp.zeros((size, size), jnp.float32)
    pg_imag = jnp.zeros((size, size), jnp.float32)
    power_sum = jnp.zeros((), jnp.float32)
    for slot in range(slots):
        row = jnp.clip(marks[2 + 2 * slot], 0, HALO)
        col = jnp.clip(marks[3 + 2 * slot], 0, HALO)
        live = slot < marks[0]
        z_real = take_window(ext, 0, row, col, size)
        z_imag = take_window(ext, 1, row, col, size)
        psi_real = p_real * z_real - p_imag * z_imag
        psi_imag = p_real * z_imag + p_imag * z_real
        plus = jnp.concatenate(
            [psi_real[:, :half] + psi_real[:, half:], psi_imag[:, :half] + psi_imag[:, half:]], axis=1
        )
        minus = jnp.concatenate(
            [psi_real[:, :half] - psi_real[:, half:], psi_imag[:, :half] - psi_imag[:, half:]], axis=1
        )
        a_even = mul3(split(plus), even)
        a_odd = mul3(split(minus), odd)
        y_real = jnp.concatenate([a_even[:, :half], a_odd[:, :half]], axis=1)
        y_imag = jnp.concatenate([a_even[:, half:], a_odd[:, half:]], axis=1)
        plus = jnp.concatenate([y_real[:half] + y_real[half:], y_imag[:half] + y_imag[half:]], axis=0)
        minus = jnp.concatenate([y_real[:half] - y_real[half:], y_imag[:half] - y_imag[half:]], axis=0)
        sums = []
        for part, (data, table, back) in enumerate(((plus, even_t, even), (minus, odd_t, odd))):
            hat = mul3(table, split(data))
            h_real = hat[:half]
            h_imag = hat[half:]
            magnitude = h_real * h_real + h_imag * h_imag
            measured = amp[slot, part * half : (part + 1) * half, :]
            ratio = measured * lax.rsqrt(magnitude + smooth_floor) - 1.0
            scaled = jnp.concatenate([h_real * ratio, h_imag * ratio], axis=0)
            sums.append(mul3(back, split(scaled)))
        top = sums[0] + sums[1]
        bottom = sums[0] - sums[1]
        z_even = jnp.concatenate(
            [
                jnp.concatenate([top[:half, :half], top[half:, :half]], axis=1),
                jnp.concatenate([bottom[:half, :half], bottom[half:, :half]], axis=1),
            ],
            axis=0,
        )
        z_odd = jnp.concatenate(
            [
                jnp.concatenate([top[:half, half:], top[half:, half:]], axis=1),
                jnp.concatenate([bottom[:half, half:], bottom[half:, half:]], axis=1),
            ],
            axis=0,
        )
        u = mul3(split(z_even), even_t)
        v = mul3(split(z_odd), odd_t)
        plus = u + v
        minus = u - v
        d_real = jnp.concatenate([plus[:, :half], minus[:, :half]], axis=1)
        d_imag = jnp.concatenate([plus[:, half:], minus[:, half:]], axis=1)
        d_real = jnp.where(live, d_real, 0.0)
        d_imag = jnp.where(live, d_imag, 0.0)
        pg_real = pg_real + (z_real * d_real + z_imag * d_imag)
        pg_imag = pg_imag + (z_real * d_imag - z_imag * d_real)
        terms[slot, 0] = (p_real * d_real + p_imag * d_imag) * scale
        terms[slot, 1] = (p_real * d_imag - p_imag * d_real) * scale
        window_power = jnp.sum(z_real * z_real + z_imag * z_imag)
        power_sum = power_sum + jnp.where(live, window_power, 0.0)

    second = marks[1] == 1
    per = 2 * size // members
    for half_at in range(2):
        columns = slice(half_at * half, (half_at + 1) * half)
        kept = jnp.where(second, pg_imag[:, columns], pg_real[:, columns])
        given = jnp.where(second, pg_real[:, columns], pg_imag[:, columns])
        for m in range(members // 2):
            at = (half_at * members // 2 + m) * (per + 2)
            for ref, value in ((keep, kept), (give, given)):
                ref[at : at + per, :] = value[m * per : (m + 1) * per, :]
                ref[at + per : at + per + 2, :] = jnp.full((2, half), power_sum)


def moved_probe(marks, probe, mine, other, power):
    size = probe.shape[1]
    second = marks[1] == 1
    factor = 1.0 / (power[0:1, 0:1] / (size * size) + tiny_value)
    p_real = probe[0]
    p_imag = probe[1]
    one = jnp.concatenate([mine[:size, :], mine[size:, :]], axis=1)
    two = jnp.concatenate([other[:size, :], other[size:, :]], axis=1)
    m_real = p_real + jnp.where(second, two, one) * factor
    m_imag = p_imag + jnp.where(second, one, two) * factor
    old = jnp.sum(p_real * p_real + p_imag * p_imag)
    new = jnp.sum(m_real * m_real + m_imag * m_imag)
    gain = jnp.sqrt(jnp.full((1, 1), old) / (jnp.full((1, 1), new) + tiny_value))
    return m_real * gain, m_imag * gain


def probe_kernel(marks, probe, mine, other, power, out):
    real, imag = moved_probe(marks, probe, mine, other, power)
    out[0] = real
    out[1] = imag


def place_kernel(marks, tile, terms, partial, rim_right, rim_low, rim_corner, ext):
    size = tile.shape[1]
    slots = terms.shape[0]
    ext[...] = jnp.zeros_like(ext)
    for slot in range(slots):
        row = jnp.clip(marks[2 + 2 * slot], 0, HALO)
        col = jnp.clip(marks[3 + 2 * slot], 0, HALO)
        for part in range(2):
            add_window(ext, part, row, col, terms[slot, part])
    partial[...] = tile[...] + ext[:, :size, :size]
    rim_right[...] = ext[:, :size, size:]
    rim_low[...] = ext[:, size : size + HALO, :size]
    rim_corner[...] = ext[:, size : size + HALO, size:]


def update_kernel(with_edges, partial, from_left, from_above, from_corner, out, *edges):
    out[...] = partial[...]
    out[:, :, :HALO] += from_left[...]
    out[:, :HALO, :] += from_above[...]
    out[:, :HALO, :HALO] += from_corner[...]
    if with_edges:
        edges_kernel(out, *edges)


def fold_kernel(members, copies, keep, source, out, *power):
    count = source.shape[0]
    n = count // members
    step = 4 * n
    groups = count // step
    total = source[0:step, :]
    for g in range(1, groups):
        total = total + source[g * step : (g + 1) * step, :]
    summed = total[0:n] + total[n : 2 * n] + (total[2 * n : 3 * n] + total[3 * n :])
    for c in range(copies):
        out[c * keep : (c + 1) * keep, :] = summed[:keep]
    if power:
        power[0][...] = jnp.broadcast_to(summed[n - 1 : n], power[0].shape)


def call(kernel, outs, specs, *args, scratch=(), grant=2):
    return pl.pallas_call(
        kernel,
        out_shape=[jax.ShapeDtypeStruct(shape, jnp.float32) for shape in outs],
        in_specs=specs,
        out_specs=[VMEM] * len(outs),
        scratch_shapes=[pltpu.VMEM(shape, jnp.float32) for shape in scratch],
        compiler_params=pltpu.CompilerParams(vmem_limit_bytes=grant << 20),
    )(*args)


def halo(edges):
    return shifted(edges[0], -1, 0), shifted(edges[1], 0, -1), shifted(edges[2], -1, -1)


def shards(object_field, probe_field, amplitudes, offsets, counts):
    _, size, _ = object_field.shape
    half = size // 2
    slots = amplitudes.shape[0]
    margin = HALO
    edge_shapes = [(2, margin, size), (2, size, margin), (2, margin, margin)]
    wide_groups, line_groups = device_groups(lax.axis_size("row"), lax.axis_size("col"))
    wide, line = len(wide_groups[0]), len(line_groups[0])
    per = 2 * size // wide
    held = wide * (per + 2)
    tables = jnp.asarray(make_tables(size))
    order = np.concatenate([np.arange(0, size, 2), np.arange(1, size, 2)])
    pick = jnp.asarray(np.eye(size)[:, order].astype(jnp.bfloat16))
    core = jnp.bitwise_and(lax.axis_index("col"), 1).astype(jnp.int32)
    marks = jnp.concatenate([counts.reshape(1), core.reshape(1), offsets.reshape(2 * slots)])

    current = object_field
    edges = call(edges_kernel, edge_shapes, [VMEM], current)
    amp, probe_now = call(
        order_kernel,
        [amplitudes.shape, probe_field.shape],
        [VMEM] * 3,
        amplitudes,
        pick,
        probe_field,
        scratch=[(2 * slots, size, half)],
    )
    low, right, corner = halo(edges)
    mine = other = power = None
    for outer_step in range(OUTER):
        first = outer_step == 0
        outs = [(held, half), (held, half), (slots, 2, size, size)]
        args = [marks, current, low, right, corner, probe_now]
        if not first:
            outs.append((2, size, size))
            args += [mine, other, power]
        args += [amp, tables]
        done = call(
            functools.partial(solve_kernel, first, wide),
            outs,
            [SMEM] + [VMEM] * (len(args) - 1),
            *args,
            scratch=[(2, size + margin + SUB, size + margin)],
            grant=8,
        )
        keep, give, terms = done[:3]
        if not first:
            probe_now = done[3]
        given = swap_cores(give)
        partial, rim_right, rim_low, rim_corner = call(
            place_kernel,
            [current.shape, edge_shapes[1], edge_shapes[0], edge_shapes[2]],
            [SMEM, VMEM, VMEM],
            marks,
            current,
            terms,
            scratch=[(2, size + margin + SUB, size + margin)],
            grant=3,
        )
        from_left = shifted(rim_right, 0, 1)
        from_above = shifted(rim_low, 1, 0)
        from_corner = shifted(rim_corner, 1, 1)
        arrived = exchange(keep + given, wide_groups)
        (copies,) = call(
            functools.partial(fold_kernel, wide, line, per + 2),
            [(line * (per + 2), half)],
            [VMEM],
            arrived,
        )
        arrived = exchange(copies, line_groups)
        copies, power = call(
            functools.partial(fold_kernel, line, wide, per),
            [(wide * per, half), (8, half)],
            [VMEM],
            arrived,
        )
        mine = exchange(copies, wide_groups)
        other = swap_cores(mine)
        last = outer_step == OUTER - 1
        current, *edges = call(
            functools.partial(update_kernel, not last),
            [current.shape] + ([] if last else edge_shapes),
            [VMEM] * 4,
            partial,
            from_left,
            from_above,
            from_corner,
        )
        if not last:
            low, right, corner = halo(edges)
    (probe_now,) = call(
        probe_kernel,
        [probe_field.shape],
        [SMEM] + [VMEM] * 4,
        marks,
        probe_now,
        mine,
        other,
        power,
    )
    return (current, probe_now)


def solution(mesh):
    return jax.shard_map(
        shards,
        mesh=mesh,
        in_specs=(
            P(None, "row", "col"),
            P(),
            P("row", "col", None),
            P("row", "col", None, None),
            P("row", "col"),
        ),
        out_specs=(P(None, "row", "col"), P()),
        check_vma=False,
    )
```

```python
import functools

import jax
import jax.numpy as jnp
import numpy as np
from jax import lax
from jax.experimental import pallas as pl
from jax.experimental.pallas import tpu as pltpu
from jax.sharding import PartitionSpec as P


HALO = 128
SUB, LANE = 8, 128
OUTER = 2
NEAR = 8

smooth_floor = 0.5
object_step = 0.5
tiny_value = 1e-06

VMEM = pl.BlockSpec(memory_space=pltpu.VMEM)
SMEM = pl.BlockSpec(memory_space=pltpu.SMEM)


def shifted(value, down_by, across_by):
    down = lax.axis_size("row")
    across = lax.axis_size("col")
    pairs = [
        (r * across + c, (r + down_by) * across + c + across_by)
        for r in range(down)
        for c in range(across)
        if 0 <= r + down_by < down and 0 <= c + across_by < across
    ]
    return lax.ppermute(value, ("row", "col"), pairs)


def device_groups(down, across):
    far = down // NEAR
    wide_groups = [
        [(y * NEAR + z) * across + x * 2 + core for y in range(far) for x in range(across // 2)]
        for z in range(NEAR)
        for core in range(2)
    ]
    line_groups = [
        [(y * NEAR + z) * across + c for z in range(NEAR)]
        for y in range(far)
        for c in range(across)
    ]
    return wide_groups, line_groups


def swap_cores(value):
    across = lax.axis_size("col")
    return lax.ppermute(value, "col", [(c, c ^ 1) for c in range(across)])


def exchange(rows, groups):
    count, lanes = rows.shape
    paired = rows.reshape(count // 2, 2, lanes)
    moved = lax.all_to_all(
        paired, ("row", "col"), 0, 0, tiled=True, axis_index_groups=groups
    )
    return moved.reshape(count, lanes)


def make_tables(length):
    half = length // 2
    out = []
    for start in (0, 1):
        first = np.arange(half)[:, None]
        second = np.arange(start, length, 2)[None, :]
        angle = -2.0 * np.pi * ((first * second) % length) / length
        real = np.cos(angle) / np.sqrt(length)
        imag = np.sin(angle) / np.sqrt(length)
        block = np.block([[real, imag], [-imag, real]])
        for table in (block, block.T):
            high = table.astype(np.float32).astype(jnp.bfloat16)
            low = (table - high.astype(np.float64)).astype(np.float32)
            out += [high, low.astype(jnp.bfloat16)]
    return np.stack(out)


def split(value):
    high = value.astype(jnp.bfloat16)
    low = (value - high.astype(jnp.float32)).astype(jnp.bfloat16)
    return high, low


def mul(left, right):
    return jnp.dot(left, right, preferred_element_type=jnp.float32)


def mul3(left, right):
    return mul(left[0], right[0]) + (mul(left[0], right[1]) + mul(left[1], right[0]))


def edges_kernel(tile, low, right, corner):
    low[...] = tile[:, :HALO, :]
    right[...] = tile[:, :, :HALO]
    corner[...] = tile[:, :HALO, :HALO]


def order_kernel(amplitudes, pick, probe, out, probe_out, held):
    slots, size, _ = amplitudes.shape
    half = size // 2
    probe_out[...] = probe[...]
    for slot in range(slots):
        rest = amplitudes[slot]
        total = jnp.zeros((size, size), jnp.float32)
        for _ in range(3):
            piece = rest.astype(jnp.bfloat16)
            total = total + mul(piece, pick[...])
            rest = rest - piece.astype(jnp.float32)
        for side in range(2):
            held[2 * slot + side] = total[:, side * half : (side + 1) * half]
            for part in range(2):
                out[slot, part * half : (part + 1) * half, side * half : (side + 1) * half] = held[
                    2 * slot + side, pl.ds(part, half, 2), :
                ]


def halves(row):
    rest = jnp.bitwise_and(row, SUB - 1)
    base = pl.multiple_of(row - rest, SUB)
    at_row = lax.broadcasted_iota(jnp.int32, (1, SUB, LANE), 1)
    at_col = lax.broadcasted_iota(jnp.int32, (1, SUB, LANE), 2)
    return rest, base, at_row, at_col


def take_window(ext, part, row, col, size):
    rest, base, at_row, at_col = halves(row)
    wide = ext[part, pl.ds(base, size + SUB), :]
    wide = wide.reshape(size // SUB + 1, SUB, wide.shape[1])
    turn_col = jnp.bitwise_and(LANE - col, LANE - 1)
    turn_row = jnp.bitwise_and(SUB - rest, SUB - 1)
    turned = []
    for t in range(wide.shape[2] // LANE):
        block = pltpu.roll(wide[:, :, t * LANE : (t + 1) * LANE], turn_col, 2)
        turned.append(pltpu.roll(block, turn_row, 1))
    out = []
    for t in range(len(turned) - 1):
        block = jnp.where(at_col < LANE - col, turned[t], turned[t + 1])
        block = jnp.where(at_row < SUB - rest, block[:-1], block[1:])
        out.append(block.reshape(size, LANE))
    return jnp.concatenate(out, axis=1)


def add_window(ext, part, row, col, value):
    size = value.shape[0]
    rest, base, at_row, at_col = halves(row)
    turn_col = jnp.bitwise_and(col, LANE - 1)
    blocks = []
    for t in range(size // LANE):
        block = value[:, t * LANE : (t + 1) * LANE].reshape(size // SUB, SUB, LANE)
        block = pltpu.roll(pltpu.roll(block, turn_col, 2), rest, 1)
        edge = jnp.zeros((1, SUB, LANE), jnp.float32)
        blocks.append(
            jnp.where(
                at_row < rest,
                jnp.concatenate([edge, block], axis=0),
                jnp.concatenate([block, edge], axis=0),
            )
        )
    none = jnp.zeros_like(blocks[0])
    blocks = [none] + blocks + [none]
    for t in range(len(blocks) - 1):
        placed = jnp.where(at_col < col, blocks[t], blocks[t + 1])
        at = (part, pl.ds(base, size + SUB), slice(t * LANE, (t + 1) * LANE))
        ext[at] = ext[at] + placed.reshape(size + SUB, LANE)


def solve_kernel(first, members, *refs):
    if first:
        (marks, tile, low, right, corner, probe, amp, tables) = refs[:8]
        keep, give, terms, ext = refs[8:]
    else:
        (marks, tile, low, right, probe, mine, other, power, amp, tables) = refs[:10]
        keep, give, terms, new_probe, ext = refs[10:]
    size = tile.shape[1]
    half = size // 2
    slots = amp.shape[0]
    ext[:, :size, :size] = tile[...]
    ext[:, :size, size:] = right[...]
    if first:
        ext[:, size : size + HALO, :size] = low[...]
        ext[:, size : size + HALO, size:] = corner[...]
    else:
        ext[:, size : size + HALO, :] = low[...]
    ext[:, size + HALO :, :] = jnp.zeros((2, SUB, size + HALO), jnp.float32)

    if first:
        p_real = probe[0]
        p_imag = probe[1]
    else:
        p_real, p_imag = moved_probe(marks, probe, mine, other, power)
        new_probe[0] = p_real
        new_probe[1] = p_imag
    mean = jnp.sum(p_real * p_real + p_imag * p_imag) / (size * size)
    scale = object_step / (mean + tiny_value)

    even, even_t, odd, odd_t = (
        (tables[2 * n], tables[2 * n + 1]) for n in range(4)
    )
    pg_real = jnp.zeros((size, size), jnp.float32)
    pg_imag = jnp.zeros((size, size), jnp.float32)
    power_sum = jnp.zeros((), jnp.float32)
    for slot in range(slots):
        row = jnp.clip(marks[2 + 2 * slot], 0, HALO)
        col = jnp.clip(marks[3 + 2 * slot], 0, HALO)
        live = slot < marks[0]
        z_real = take_window(ext, 0, row, col, size)
        z_imag = take_window(ext, 1, row, col, size)
        psi_real = p_real * z_real - p_imag * z_imag
        psi_imag = p_real * z_imag + p_imag * z_real
        plus = jnp.concatenate(
            [psi_real[:, :half] + psi_real[:, half:], psi_imag[:, :half] + psi_imag[:, half:]], axis=1
        )
        minus = jnp.concatenate(
            [psi_real[:, :half] - psi_real[:, half:], psi_imag[:, :half] - psi_imag[:, half:]], axis=1
        )
        a_even = mul3(split(plus), even)
        a_odd = mul3(split(minus), odd)
        y_real = jnp.concatenate([a_even[:, :half], a_odd[:, :half]], axis=1)
        y_imag = jnp.concatenate([a_even[:, half:], a_odd[:, half:]], axis=1)
        plus = jnp.concatenate([y_real[:half] + y_real[half:], y_imag[:half] + y_imag[half:]], axis=0)
        minus = jnp.concatenate([y_real[:half] - y_real[half:], y_imag[:half] - y_imag[half:]], axis=0)
        sums = []
        for part, (data, table, back) in enumerate(((plus, even_t, even), (minus, odd_t, odd))):
            hat = mul3(table, split(data))
            h_real = hat[:half]
            h_imag = hat[half:]
            magnitude = h_real * h_real + h_imag * h_imag
            measured = amp[slot, part * half : (part + 1) * half, :]
            ratio = measured * lax.rsqrt(magnitude + smooth_floor) - 1.0
            scaled = jnp.concatenate([h_real * ratio, h_imag * ratio], axis=0)
            sums.append(mul3(back, split(scaled)))
        top = sums[0] + sums[1]
        bottom = sums[0] - sums[1]
        z_even = jnp.concatenate(
            [
                jnp.concatenate([top[:half, :half], top[half:, :half]], axis=1),
                jnp.concatenate([bottom[:half, :half], bottom[half:, :half]], axis=1),
            ],
            axis=0,
        )
        z_odd = jnp.concatenate(
            [
                jnp.concatenate([top[:half, half:], top[half:, half:]], axis=1),
                jnp.concatenate([bottom[:half, half:], bottom[half:, half:]], axis=1),
            ],
            axis=0,
        )
        u = mul3(split(z_even), even_t)
        v = mul3(split(z_odd), odd_t)
        plus = u + v
        minus = u - v
        d_real = jnp.concatenate([plus[:, :half], minus[:, :half]], axis=1)
        d_imag = jnp.concatenate([plus[:, half:], minus[:, half:]], axis=1)
        d_real = jnp.where(live, d_real, 0.0)
        d_imag = jnp.where(live, d_imag, 0.0)
        pg_real = pg_real + (z_real * d_real + z_imag * d_imag)
        pg_imag = pg_imag + (z_real * d_imag - z_imag * d_real)
        terms[slot, 0] = (p_real * d_real + p_imag * d_imag) * scale
        terms[slot, 1] = (p_real * d_imag - p_imag * d_real) * scale
        window_power = jnp.sum(z_real * z_real + z_imag * z_imag)
        power_sum = power_sum + jnp.where(live, window_power, 0.0)

    second = marks[1] == 1
    per = 2 * size // members
    for half_at in range(2):
        columns = slice(half_at * half, (half_at + 1) * half)
        kept = jnp.where(second, pg_imag[:, columns], pg_real[:, columns])
        given = jnp.where(second, pg_real[:, columns], pg_imag[:, columns])
        for m in range(members // 2):
            at = (half_at * members // 2 + m) * (per + 2)
            for ref, value in ((keep, kept), (give, given)):
                ref[at : at + per, :] = value[m * per : (m + 1) * per, :]
                ref[at + per : at + per + 2, :] = jnp.full((2, half), power_sum)


def moved_probe(marks, probe, mine, other, power):
    size = probe.shape[1]
    second = marks[1] == 1
    factor = 1.0 / (power[0:1, 0:1] / (size * size) + tiny_value)
    p_real = probe[0]
    p_imag = probe[1]
    one = jnp.concatenate([mine[:size, :], mine[size:, :]], axis=1)
    two = jnp.concatenate([other[:size, :], other[size:, :]], axis=1)
    m_real = p_real + jnp.where(second, two, one) * factor
    m_imag = p_imag + jnp.where(second, one, two) * factor
    old = jnp.sum(p_real * p_real + p_imag * p_imag)
    new = jnp.sum(m_real * m_real + m_imag * m_imag)
    gain = jnp.sqrt(jnp.full((1, 1), old) / (jnp.full((1, 1), new) + tiny_value))
    return m_real * gain, m_imag * gain


def probe_kernel(marks, probe, mine, other, power, out):
    real, imag = moved_probe(marks, probe, mine, other, power)
    out[0] = real
    out[1] = imag


def place_kernel(marks, tile, terms, partial, rim_right, rim_low, rim_corner, ext):
    size = tile.shape[1]
    slots = terms.shape[0]
    ext[...] = jnp.zeros_like(ext)
    for slot in range(slots):
        row = jnp.clip(marks[2 + 2 * slot], 0, HALO)
        col = jnp.clip(marks[3 + 2 * slot], 0, HALO)
        for part in range(2):
            add_window(ext, part, row, col, terms[slot, part])
    partial[...] = tile[...] + ext[:, :size, :size]
    rim_right[...] = ext[:, :size, size:]
    rim_low[...] = ext[:, size : size + HALO, :size]
    rim_corner[...] = ext[:, size : size + HALO, size:]


def update_kernel(partial, from_left, from_above, from_corner, out, *side):
    out[...] = partial[...]
    out[:, :, :HALO] += from_left[...]
    out[:, :HALO, :] += from_above[...]
    out[:, :HALO, :HALO] += from_corner[...]
    if side:
        side[0][...] = out[:, :, :HALO]


def join_kernel(tile, right, out):
    size = tile.shape[1]
    out[:, :, :size] = tile[:, :HALO, :]
    out[:, :, size:] = right[:, :HALO, :]


def fold_kernel(members, copies, keep, source, out, *power):
    count = source.shape[0]
    n = count // members
    step = 4 * n
    groups = count // step
    total = source[0:step, :]
    for g in range(1, groups):
        total = total + source[g * step : (g + 1) * step, :]
    summed = total[0:n] + total[n : 2 * n] + (total[2 * n : 3 * n] + total[3 * n :])
    for c in range(copies):
        out[c * keep : (c + 1) * keep, :] = summed[:keep]
    if power:
        power[0][...] = jnp.broadcast_to(summed[n - 1 : n], power[0].shape)


def call(kernel, outs, specs, *args, scratch=(), grant=2):
    return pl.pallas_call(
        kernel,
        out_shape=[jax.ShapeDtypeStruct(shape, jnp.float32) for shape in outs],
        in_specs=specs,
        out_specs=[VMEM] * len(outs),
        scratch_shapes=[pltpu.VMEM(shape, jnp.float32) for shape in scratch],
        compiler_params=pltpu.CompilerParams(vmem_limit_bytes=grant << 20),
    )(*args)


def shards(object_field, probe_field, amplitudes, offsets, counts):
    _, size, _ = object_field.shape
    half = size // 2
    slots = amplitudes.shape[0]
    margin = HALO
    edge_shapes = [(2, margin, size), (2, size, margin), (2, margin, margin)]
    wide_groups, line_groups = device_groups(lax.axis_size("row"), lax.axis_size("col"))
    wide, line = len(wide_groups[0]), len(line_groups[0])
    per = 2 * size // wide
    held = wide * (per + 2)
    tables = jnp.asarray(make_tables(size))
    order = np.concatenate([np.arange(0, size, 2), np.arange(1, size, 2)])
    pick = jnp.asarray(np.eye(size)[:, order].astype(jnp.bfloat16))
    core = jnp.bitwise_and(lax.axis_index("col"), 1).astype(jnp.int32)
    marks = jnp.concatenate([counts.reshape(1), core.reshape(1), offsets.reshape(2 * slots)])

    current = object_field
    edges = call(edges_kernel, edge_shapes, [VMEM], current)
    amp, probe_now = call(
        order_kernel,
        [amplitudes.shape, probe_field.shape],
        [VMEM] * 3,
        amplitudes,
        pick,
        probe_field,
        scratch=[(2 * slots, size, half)],
    )
    low = shifted(edges[0], -1, 0)
    right = shifted(edges[1], 0, -1)
    corner = shifted(edges[2], -1, -1)
    mine = other = power = None
    for outer_step in range(OUTER):
        first = outer_step == 0
        outs = [(held, half), (held, half), (slots, 2, size, size)]
        args = [marks, current, low, right] + ([corner] if first else []) + [probe_now]
        if not first:
            outs.append((2, size, size))
            args += [mine, other, power]
        args += [amp, tables]
        done = call(
            functools.partial(solve_kernel, first, wide),
            outs,
            [SMEM] + [VMEM] * (len(args) - 1),
            *args,
            scratch=[(2, size + margin + SUB, size + margin)],
            grant=8,
        )
        keep, give, terms = done[:3]
        if not first:
            probe_now = done[3]
        given = swap_cores(give)
        partial, rim_right, rim_low, rim_corner = call(
            place_kernel,
            [current.shape, edge_shapes[1], edge_shapes[0], edge_shapes[2]],
            [SMEM, VMEM, VMEM],
            marks,
            current,
            terms,
            scratch=[(2, size + margin + SUB, size + margin)],
            grant=3,
        )
        from_left = shifted(rim_right, 0, 1)
        from_above = shifted(rim_low, 1, 0)
        from_corner = shifted(rim_corner, 1, 1)
        arrived = exchange(keep + given, wide_groups)
        (copies,) = call(
            functools.partial(fold_kernel, wide, line, per + 2),
            [(line * (per + 2), half)],
            [VMEM],
            arrived,
        )
        arrived = exchange(copies, line_groups)
        copies, power = call(
            functools.partial(fold_kernel, line, wide, per),
            [(wide * per, half), (8, half)],
            [VMEM],
            arrived,
        )
        mine = exchange(copies, wide_groups)
        other = swap_cores(mine)
        last = outer_step == OUTER - 1
        current, *side = call(
            update_kernel,
            [current.shape] + ([] if last else [edge_shapes[1]]),
            [VMEM] * 4,
            partial,
            from_left,
            from_above,
            from_corner,
        )
        if not last:
            right = shifted(side[0], 0, -1)
            (joined,) = call(join_kernel, [(2, margin, size + margin)], [VMEM] * 2, current, right)
            low = shifted(joined, -1, 0)
    (probe_now,) = call(
        probe_kernel,
        [probe_field.shape],
        [SMEM] + [VMEM] * 4,
        marks,
        probe_now,
        mine,
        other,
        power,
    )
    return (current, probe_now)


def solution(mesh):
    return jax.shard_map(
        shards,
        mesh=mesh,
        in_specs=(
            P(None, "row", "col"),
            P(),
            P("row", "col", None),
            P("row", "col", None, None),
            P("row", "col"),
        ),
        out_specs=(P(None, "row", "col"), P()),
        check_vma=False,
    )
```

```python
import functools

import jax
import jax.numpy as jnp
import numpy as np
from jax import lax
from jax.experimental import pallas as pl
from jax.experimental.pallas import tpu as pltpu
from jax.sharding import PartitionSpec as P


HALO = 128
SUB, LANE = 8, 128
OUTER = 2
NEAR = 8

smooth_floor = 0.5
object_step = 0.5
tiny_value = 1e-06

VMEM = pl.BlockSpec(memory_space=pltpu.VMEM)
SMEM = pl.BlockSpec(memory_space=pltpu.SMEM)


def shifted(value, down_by, across_by):
    down = lax.axis_size("row")
    across = lax.axis_size("col")
    pairs = [
        (r * across + c, (r + down_by) * across + c + across_by)
        for r in range(down)
        for c in range(across)
        if 0 <= r + down_by < down and 0 <= c + across_by < across
    ]
    return lax.ppermute(value, ("row", "col"), pairs)


def device_groups(down, across):
    far = down // NEAR
    wide_groups = [
        [(y * NEAR + z) * across + x * 2 + core for y in range(far) for x in range(across // 2)]
        for z in range(NEAR)
        for core in range(2)
    ]
    line_groups = [
        [(y * NEAR + z) * across + c for z in range(NEAR)]
        for y in range(far)
        for c in range(across)
    ]
    return wide_groups, line_groups


def swap_cores(value):
    across = lax.axis_size("col")
    return lax.ppermute(value, "col", [(c, c ^ 1) for c in range(across)])


def exchange(rows, groups):
    count, lanes = rows.shape
    paired = rows.reshape(count // 2, 2, lanes)
    moved = lax.all_to_all(
        paired, ("row", "col"), 0, 0, tiled=True, axis_index_groups=groups
    )
    return moved.reshape(count, lanes)


def make_tables(length):
    half = length // 2
    out = []
    for start in (0, 1):
        first = np.arange(half)[:, None]
        second = np.arange(start, length, 2)[None, :]
        angle = -2.0 * np.pi * ((first * second) % length) / length
        real = np.cos(angle) / np.sqrt(length)
        imag = np.sin(angle) / np.sqrt(length)
        block = np.block([[real, imag], [-imag, real]])
        for table in (block, block.T):
            high = table.astype(np.float32).astype(jnp.bfloat16)
            low = (table - high.astype(np.float64)).astype(np.float32)
            out += [high, low.astype(jnp.bfloat16)]
    return np.stack(out)


def split(value):
    high = value.astype(jnp.bfloat16)
    low = (value - high.astype(jnp.float32)).astype(jnp.bfloat16)
    return high, low


def mul(left, right):
    return jnp.dot(left, right, preferred_element_type=jnp.float32)


def mul3(left, right):
    return mul(left[0], right[0]) + (mul(left[0], right[1]) + mul(left[1], right[0]))


def edges_kernel(tile, low, right, corner):
    low[...] = tile[:, :HALO, :]
    right[...] = tile[:, :, :HALO]
    corner[...] = tile[:, :HALO, :HALO]


def order_kernel(amplitudes, pick, probe, out, probe_out, held):
    slots, size, _ = amplitudes.shape
    half = size // 2
    probe_out[...] = probe[...]
    for slot in range(slots):
        rest = amplitudes[slot]
        total = jnp.zeros((size, size), jnp.float32)
        for _ in range(3):
            piece = rest.astype(jnp.bfloat16)
            total = total + mul(piece, pick[...])
            rest = rest - piece.astype(jnp.float32)
        for side in range(2):
            held[2 * slot + side] = total[:, side * half : (side + 1) * half]
            for part in range(2):
                out[slot, part * half : (part + 1) * half, side * half : (side + 1) * half] = held[
                    2 * slot + side, pl.ds(part, half, 2), :
                ]


def halves(row):
    rest = jnp.bitwise_and(row, SUB - 1)
    base = pl.multiple_of(row - rest, SUB)
    at_row = lax.broadcasted_iota(jnp.int32, (1, SUB, LANE), 1)
    at_col = lax.broadcasted_iota(jnp.int32, (1, SUB, LANE), 2)
    return rest, base, at_row, at_col


def take_window(ext, part, row, col, size):
    rest, base, at_row, at_col = halves(row)
    wide = ext[part, pl.ds(base, size + SUB), :]
    wide = wide.reshape(size // SUB + 1, SUB, wide.shape[1])
    turn_col = jnp.bitwise_and(LANE - col, LANE - 1)
    turn_row = jnp.bitwise_and(SUB - rest, SUB - 1)
    turned = []
    for t in range(wide.shape[2] // LANE):
        block = pltpu.roll(wide[:, :, t * LANE : (t + 1) * LANE], turn_col, 2)
        turned.append(pltpu.roll(block, turn_row, 1))
    out = []
    for t in range(len(turned) - 1):
        block = jnp.where(at_col < LANE - col, turned[t], turned[t + 1])
        block = jnp.where(at_row < SUB - rest, block[:-1], block[1:])
        out.append(block.reshape(size, LANE))
    return jnp.concatenate(out, axis=1)


def add_window(ext, part, row, col, value):
    size = value.shape[0]
    rest, base, at_row, at_col = halves(row)
    turn_col = jnp.bitwise_and(col, LANE - 1)
    blocks = []
    for t in range(size // LANE):
        block = value[:, t * LANE : (t + 1) * LANE].reshape(size // SUB, SUB, LANE)
        block = pltpu.roll(pltpu.roll(block, turn_col, 2), rest, 1)
        edge = jnp.zeros((1, SUB, LANE), jnp.float32)
        blocks.append(
            jnp.where(
                at_row < rest,
                jnp.concatenate([edge, block], axis=0),
                jnp.concatenate([block, edge], axis=0),
            )
        )
    none = jnp.zeros_like(blocks[0])
    blocks = [none] + blocks + [none]
    for t in range(len(blocks) - 1):
        placed = jnp.where(at_col < col, blocks[t], blocks[t + 1])
        at = (part, pl.ds(base, size + SUB), slice(t * LANE, (t + 1) * LANE))
        ext[at] = ext[at] + placed.reshape(size + SUB, LANE)


def solve_kernel(first, members, *refs):
    if first:
        (marks, tile, low, right, corner, probe, amp, tables) = refs[:8]
        keep, give, terms, ext = refs[8:]
    else:
        (marks, tile, low, right, probe, mine, other, power, amp, tables) = refs[:10]
        keep, give, terms, new_probe, ext = refs[10:]
    size = tile.shape[1]
    half = size // 2
    slots = amp.shape[0]
    ext[:, :size, :size] = tile[...]
    ext[:, :size, size:] = right[...]
    if first:
        ext[:, size : size + HALO, :size] = low[...]
        ext[:, size : size + HALO, size:] = corner[...]
    else:
        ext[:, size : size + HALO, :] = low[...]
    ext[:, size + HALO :, :] = jnp.zeros((2, SUB, size + HALO), jnp.float32)

    if first:
        p_real = probe[0]
        p_imag = probe[1]
    else:
        p_real, p_imag = moved_probe(marks, probe, mine, other, power)
        new_probe[0] = p_real
        new_probe[1] = p_imag
    mean = jnp.sum(p_real * p_real + p_imag * p_imag) / (size * size)
    scale = object_step / (mean + tiny_value)

    even, even_t, odd, odd_t = (
        (tables[2 * n], tables[2 * n + 1]) for n in range(4)
    )
    pg_real = jnp.zeros((size, size), jnp.float32)
    pg_imag = jnp.zeros((size, size), jnp.float32)
    power_sum = jnp.zeros((), jnp.float32)
    for slot in range(slots):
        row = jnp.clip(marks[2 + 2 * slot], 0, HALO)
        col = jnp.clip(marks[3 + 2 * slot], 0, HALO)
        live = slot < marks[0]
        z_real = take_window(ext, 0, row, col, size)
        z_imag = take_window(ext, 1, row, col, size)
        psi_real = p_real * z_real - p_imag * z_imag
        psi_imag = p_real * z_imag + p_imag * z_real
        plus = jnp.concatenate(
            [psi_real[:, :half] + psi_real[:, half:], psi_imag[:, :half] + psi_imag[:, half:]], axis=1
        )
        minus = jnp.concatenate(
            [psi_real[:, :half] - psi_real[:, half:], psi_imag[:, :half] - psi_imag[:, half:]], axis=1
        )
        a_even = mul3(split(plus), even)
        a_odd = mul3(split(minus), odd)
        y_real = jnp.concatenate([a_even[:, :half], a_odd[:, :half]], axis=1)
        y_imag = jnp.concatenate([a_even[:, half:], a_odd[:, half:]], axis=1)
        plus = jnp.concatenate([y_real[:half] + y_real[half:], y_imag[:half] + y_imag[half:]], axis=0)
        minus = jnp.concatenate([y_real[:half] - y_real[half:], y_imag[:half] - y_imag[half:]], axis=0)
        sums = []
        for part, (data, table, back) in enumerate(((plus, even_t, even), (minus, odd_t, odd))):
            hat = mul3(table, split(data))
            h_real = hat[:half]
            h_imag = hat[half:]
            magnitude = h_real * h_real + h_imag * h_imag
            measured = amp[slot, part * half : (part + 1) * half, :]
            ratio = measured * lax.rsqrt(magnitude + smooth_floor) - 1.0
            scaled = jnp.concatenate([h_real * ratio, h_imag * ratio], axis=0)
            sums.append(mul3(back, split(scaled)))
        top = sums[0] + sums[1]
        bottom = sums[0] - sums[1]
        z_even = jnp.concatenate(
            [
                jnp.concatenate([top[:half, :half], top[half:, :half]], axis=1),
                jnp.concatenate([bottom[:half, :half], bottom[half:, :half]], axis=1),
            ],
            axis=0,
        )
        z_odd = jnp.concatenate(
            [
                jnp.concatenate([top[:half, half:], top[half:, half:]], axis=1),
                jnp.concatenate([bottom[:half, half:], bottom[half:, half:]], axis=1),
            ],
            axis=0,
        )
        u = mul3(split(z_even), even_t)
        v = mul3(split(z_odd), odd_t)
        plus = u + v
        minus = u - v
        d_real = jnp.concatenate([plus[:, :half], minus[:, :half]], axis=1)
        d_imag = jnp.concatenate([plus[:, half:], minus[:, half:]], axis=1)
        d_real = jnp.where(live, d_real, 0.0)
        d_imag = jnp.where(live, d_imag, 0.0)
        pg_real = pg_real + (z_real * d_real + z_imag * d_imag)
        pg_imag = pg_imag + (z_real * d_imag - z_imag * d_real)
        terms[slot, 0] = (p_real * d_real + p_imag * d_imag) * scale
        terms[slot, 1] = (p_real * d_imag - p_imag * d_real) * scale
        window_power = jnp.sum(z_real * z_real + z_imag * z_imag)
        power_sum = power_sum + jnp.where(live, window_power, 0.0)

    second = marks[1] == 1
    per = 2 * size // members
    for half_at in range(2):
        columns = slice(half_at * half, (half_at + 1) * half)
        kept = jnp.where(second, pg_imag[:, columns], pg_real[:, columns])
        given = jnp.where(second, pg_real[:, columns], pg_imag[:, columns])
        for m in range(members // 2):
            at = (half_at * members // 2 + m) * (per + 2)
            for ref, value in ((keep, kept), (give, given)):
                ref[at : at + per, :] = value[m * per : (m + 1) * per, :]
                ref[at + per : at + per + 2, :] = jnp.full((2, half), power_sum)


def moved_probe(marks, probe, mine, other, power):
    size = probe.shape[1]
    second = marks[1] == 1
    factor = 1.0 / (power[0:1, 0:1] / (size * size) + tiny_value)
    p_real = probe[0]
    p_imag = probe[1]
    one = jnp.concatenate([mine[:size, :], mine[size:, :]], axis=1)
    two = jnp.concatenate([other[:size, :], other[size:, :]], axis=1)
    m_real = p_real + jnp.where(second, two, one) * factor
    m_imag = p_imag + jnp.where(second, one, two) * factor
    old = jnp.sum(p_real * p_real + p_imag * p_imag)
    new = jnp.sum(m_real * m_real + m_imag * m_imag)
    gain = jnp.sqrt(jnp.full((1, 1), old) / (jnp.full((1, 1), new) + tiny_value))
    return m_real * gain, m_imag * gain


def probe_kernel(marks, probe, mine, other, power, out):
    real, imag = moved_probe(marks, probe, mine, other, power)
    out[0] = real
    out[1] = imag


def place_kernel(marks, tile, terms, partial, rim_right, rim_low, *rest):
    ext = rest[-1]
    size = tile.shape[1]
    slots = terms.shape[0]
    ext[...] = jnp.zeros_like(ext)
    for slot in range(slots):
        row = jnp.clip(marks[2 + 2 * slot], 0, HALO)
        col = jnp.clip(marks[3 + 2 * slot], 0, HALO)
        for part in range(2):
            add_window(ext, part, row, col, terms[slot, part])
    partial[...] = tile[...] + ext[:, :size, :size]
    rim_right[...] = ext[:, : rim_right.shape[1], size:]
    rim_low[...] = ext[:, size : size + HALO, :size]
    if len(rest) > 1:
        rest[0][...] = ext[:, size : size + HALO, size:]


def update_kernel(partial, from_left, from_above, from_corner, out, side):
    out[...] = partial[...]
    out[:, :, :HALO] += from_left[...]
    out[:, :HALO, :] += from_above[...]
    out[:, :HALO, :HALO] += from_corner[...]
    side[...] = out[:, :, :HALO]


def merge_kernel(rim_low, from_left, out):
    size = rim_low.shape[2]
    out[...] = rim_low[...]
    out[:, :, :HALO] += from_left[:, size:, :]


def finish_kernel(partial, from_left, from_above, out):
    size = partial.shape[1]
    out[...] = partial[...]
    out[:, :, :HALO] += from_left[:, :size, :]
    out[:, :HALO, :] += from_above[...]


def join_kernel(tile, right, out):
    size = tile.shape[1]
    out[:, :, :size] = tile[:, :HALO, :]
    out[:, :, size:] = right[:, :HALO, :]


def fold_kernel(members, copies, keep, source, out, *power):
    count = source.shape[0]
    n = count // members
    step = 4 * n
    groups = count // step
    total = source[0:step, :]
    for g in range(1, groups):
        total = total + source[g * step : (g + 1) * step, :]
    summed = total[0:n] + total[n : 2 * n] + (total[2 * n : 3 * n] + total[3 * n :])
    for c in range(copies):
        out[c * keep : (c + 1) * keep, :] = summed[:keep]
    if power:
        power[0][...] = jnp.broadcast_to(summed[n - 1 : n], power[0].shape)


def call(kernel, outs, specs, *args, scratch=(), grant=2):
    return pl.pallas_call(
        kernel,
        out_shape=[jax.ShapeDtypeStruct(shape, jnp.float32) for shape in outs],
        in_specs=specs,
        out_specs=[VMEM] * len(outs),
        scratch_shapes=[pltpu.VMEM(shape, jnp.float32) for shape in scratch],
        compiler_params=pltpu.CompilerParams(vmem_limit_bytes=grant << 20),
    )(*args)


def shards(object_field, probe_field, amplitudes, offsets, counts):
    _, size, _ = object_field.shape
    half = size // 2
    slots = amplitudes.shape[0]
    margin = HALO
    edge_shapes = [(2, margin, size), (2, size, margin), (2, margin, margin)]
    wide_groups, line_groups = device_groups(lax.axis_size("row"), lax.axis_size("col"))
    wide, line = len(wide_groups[0]), len(line_groups[0])
    per = 2 * size // wide
    held = wide * (per + 2)
    tables = jnp.asarray(make_tables(size))
    order = np.concatenate([np.arange(0, size, 2), np.arange(1, size, 2)])
    pick = jnp.asarray(np.eye(size)[:, order].astype(jnp.bfloat16))
    core = jnp.bitwise_and(lax.axis_index("col"), 1).astype(jnp.int32)
    marks = jnp.concatenate([counts.reshape(1), core.reshape(1), offsets.reshape(2 * slots)])

    current = object_field
    edges = call(edges_kernel, edge_shapes, [VMEM], current)
    amp, probe_now = call(
        order_kernel,
        [amplitudes.shape, probe_field.shape],
        [VMEM] * 3,
        amplitudes,
        pick,
        probe_field,
        scratch=[(2 * slots, size, half)],
    )
    low = shifted(edges[0], -1, 0)
    right = shifted(edges[1], 0, -1)
    corner = shifted(edges[2], -1, -1)
    mine = other = power = None
    for outer_step in range(OUTER):
        first = outer_step == 0
        outs = [(held, half), (held, half), (slots, 2, size, size)]
        args = [marks, current, low, right] + ([corner] if first else []) + [probe_now]
        if not first:
            outs.append((2, size, size))
            args += [mine, other, power]
        args += [amp, tables]
        done = call(
            functools.partial(solve_kernel, first, wide),
            outs,
            [SMEM] + [VMEM] * (len(args) - 1),
            *args,
            scratch=[(2, size + margin + SUB, size + margin)],
            grant=8,
        )
        keep, give, terms = done[:3]
        if not first:
            probe_now = done[3]
        given = swap_cores(give)
        last = outer_step == OUTER - 1
        if last:
            rim_shapes = [(2, size + margin, margin), edge_shapes[0]]
        else:
            rim_shapes = [edge_shapes[1], edge_shapes[0], edge_shapes[2]]
        partial, rim_right, rim_low, *rim_corner = call(
            place_kernel,
            [current.shape] + rim_shapes,
            [SMEM, VMEM, VMEM],
            marks,
            current,
            terms,
            scratch=[(2, size + margin + SUB, size + margin)],
            grant=3,
        )
        from_left = shifted(rim_right, 0, 1)
        if not last:
            from_above = shifted(rim_low, 1, 0)
            from_corner = shifted(rim_corner[0], 1, 1)
        if last:
            (merged,) = call(
                merge_kernel, [edge_shapes[0]], [VMEM] * 2, rim_low, from_left
            )
            from_above = shifted(merged, 1, 0)
        arrived = exchange(keep + given, wide_groups)
        (copies,) = call(
            functools.partial(fold_kernel, wide, line, per + 2),
            [(line * (per + 2), half)],
            [VMEM],
            arrived,
        )
        arrived = exchange(copies, line_groups)
        copies, power = call(
            functools.partial(fold_kernel, line, wide, per),
            [(wide * per, half), (8, half)],
            [VMEM],
            arrived,
        )
        mine = exchange(copies, wide_groups)
        other = swap_cores(mine)
        if last:
            (current,) = call(
                finish_kernel,
                [current.shape],
                [VMEM] * 3,
                partial,
                from_left,
                from_above,
            )
        else:
            current, side = call(
                update_kernel,
                [current.shape, edge_shapes[1]],
                [VMEM] * 4,
                partial,
                from_left,
                from_above,
                from_corner,
            )
            right = shifted(side, 0, -1)
            (joined,) = call(join_kernel, [(2, margin, size + margin)], [VMEM] * 2, current, right)
            low = shifted(joined, -1, 0)
    (probe_now,) = call(
        probe_kernel,
        [probe_field.shape],
        [SMEM] + [VMEM] * 4,
        marks,
        probe_now,
        mine,
        other,
        power,
    )
    return (current, probe_now)


def solution(mesh):
    return jax.shard_map(
        shards,
        mesh=mesh,
        in_specs=(
            P(None, "row", "col"),
            P(),
            P("row", "col", None),
            P("row", "col", None, None),
            P("row", "col"),
        ),
        out_specs=(P(None, "row", "col"), P()),
        check_vma=False,
    )
```

```python
import functools

import jax
import jax.numpy as jnp
import numpy as np
from jax import lax
from jax.experimental import pallas as pl
from jax.experimental.pallas import tpu as pltpu
from jax.sharding import PartitionSpec as P


HALO = 128
SUB, LANE = 8, 128
OUTER = 2
NEAR = 8

smooth_floor = 0.5
object_step = 0.5
tiny_value = 1e-06

VMEM = pl.BlockSpec(memory_space=pltpu.VMEM)
SMEM = pl.BlockSpec(memory_space=pltpu.SMEM)


def shifted(value, down_by, across_by):
    down = lax.axis_size("row")
    across = lax.axis_size("col")
    pairs = [
        (r * across + c, (r + down_by) * across + c + across_by)
        for r in range(down)
        for c in range(across)
        if 0 <= r + down_by < down and 0 <= c + across_by < across
    ]
    return lax.ppermute(value, ("row", "col"), pairs)


def device_groups(down, across):
    far = down // NEAR
    wide_groups = [
        [(y * NEAR + z) * across + x * 2 + core for y in range(far) for x in range(across // 2)]
        for z in range(NEAR)
        for core in range(2)
    ]
    line_groups = [
        [(y * NEAR + z) * across + c for z in range(NEAR)]
        for y in range(far)
        for c in range(across)
    ]
    return wide_groups, line_groups


def swap_cores(value):
    across = lax.axis_size("col")
    return lax.ppermute(value, "col", [(c, c ^ 1) for c in range(across)])


def exchange(rows, groups):
    count, lanes = rows.shape
    paired = rows.reshape(count // 2, 2, lanes)
    moved = lax.all_to_all(
        paired, ("row", "col"), 0, 0, tiled=True, axis_index_groups=groups
    )
    return moved.reshape(count, lanes)


def make_tables(length):
    half = length // 2
    out = []
    for start in (0, 1):
        first = np.arange(half)[:, None]
        second = np.arange(start, length, 2)[None, :]
        angle = -2.0 * np.pi * ((first * second) % length) / length
        real = np.cos(angle) / np.sqrt(length)
        imag = np.sin(angle) / np.sqrt(length)
        block = np.block([[real, imag], [-imag, real]])
        for table in (block, block.T):
            high = table.astype(np.float32).astype(jnp.bfloat16)
            low = (table - high.astype(np.float64)).astype(np.float32)
            out += [high, low.astype(jnp.bfloat16)]
    return np.stack(out)


def split(value):
    high = value.astype(jnp.bfloat16)
    low = (value - high.astype(jnp.float32)).astype(jnp.bfloat16)
    return high, low


def mul(left, right):
    return jnp.dot(left, right, preferred_element_type=jnp.float32)


def mul3(left, right):
    return mul(left[0], right[0]) + (mul(left[0], right[1]) + mul(left[1], right[0]))


def edges_kernel(tile, low, right, corner):
    low[...] = tile[:, :HALO, :]
    right[...] = tile[:, :, :HALO]
    corner[...] = tile[:, :HALO, :HALO]


def order_kernel(amplitudes, pick, probe, out, probe_out, held):
    slots, size, _ = amplitudes.shape
    half = size // 2
    probe_out[...] = probe[...]
    for slot in range(slots):
        rest = amplitudes[slot]
        total = jnp.zeros((size, size), jnp.float32)
        for _ in range(3):
            piece = rest.astype(jnp.bfloat16)
            total = total + mul(piece, pick[...])
            rest = rest - piece.astype(jnp.float32)
        for side in range(2):
            held[2 * slot + side] = total[:, side * half : (side + 1) * half]
            for part in range(2):
                out[slot, part * half : (part + 1) * half, side * half : (side + 1) * half] = held[
                    2 * slot + side, pl.ds(part, half, 2), :
                ]


def halves(row):
    rest = jnp.bitwise_and(row, SUB - 1)
    base = pl.multiple_of(row - rest, SUB)
    at_row = lax.broadcasted_iota(jnp.int32, (1, SUB, LANE), 1)
    at_col = lax.broadcasted_iota(jnp.int32, (1, SUB, LANE), 2)
    return rest, base, at_row, at_col


def take_window(ext, part, row, col, size):
    rest, base, at_row, at_col = halves(row)
    wide = ext[part, pl.ds(base, size + SUB), :]
    wide = wide.reshape(size // SUB + 1, SUB, wide.shape[1])
    turn_col = jnp.bitwise_and(LANE - col, LANE - 1)
    turn_row = jnp.bitwise_and(SUB - rest, SUB - 1)
    turned = []
    for t in range(wide.shape[2] // LANE):
        block = pltpu.roll(wide[:, :, t * LANE : (t + 1) * LANE], turn_col, 2)
        turned.append(pltpu.roll(block, turn_row, 1))
    out = []
    for t in range(len(turned) - 1):
        block = jnp.where(at_col < LANE - col, turned[t], turned[t + 1])
        block = jnp.where(at_row < SUB - rest, block[:-1], block[1:])
        out.append(block.reshape(size, LANE))
    return jnp.concatenate(out, axis=1)


def add_window(ext, part, row, col, value):
    size = value.shape[0]
    rest, base, at_row, at_col = halves(row)
    turn_col = jnp.bitwise_and(col, LANE - 1)
    blocks = []
    for t in range(size // LANE):
        block = value[:, t * LANE : (t + 1) * LANE].reshape(size // SUB, SUB, LANE)
        block = pltpu.roll(pltpu.roll(block, turn_col, 2), rest, 1)
        edge = jnp.zeros((1, SUB, LANE), jnp.float32)
        blocks.append(
            jnp.where(
                at_row < rest,
                jnp.concatenate([edge, block], axis=0),
                jnp.concatenate([block, edge], axis=0),
            )
        )
    none = jnp.zeros_like(blocks[0])
    blocks = [none] + blocks + [none]
    for t in range(len(blocks) - 1):
        placed = jnp.where(at_col < col, blocks[t], blocks[t + 1])
        at = (part, pl.ds(base, size + SUB), slice(t * LANE, (t + 1) * LANE))
        ext[at] = ext[at] + placed.reshape(size + SUB, LANE)


def solve_kernel(first, members, *refs):
    if first:
        (marks, tile, low, right, corner, probe, amp, tables) = refs[:8]
        keep, give, terms, ext = refs[8:]
    else:
        (marks, tile, low, right, probe, mine, other, power, amp, tables) = refs[:10]
        keep, give, terms, new_probe, ext = refs[10:]
    size = tile.shape[1]
    half = size // 2
    slots = amp.shape[0]
    ext[:, :size, :size] = tile[...]
    ext[:, size : size + HALO, :size] = low[...]
    if first:
        ext[:, :size, size:] = right[...]
        ext[:, size : size + HALO, size:] = corner[...]
    else:
        ext[:, : size + HALO, size:] = right[...]
    ext[:, size + HALO :, :] = jnp.zeros((2, SUB, size + HALO), jnp.float32)

    if first:
        p_real = probe[0]
        p_imag = probe[1]
    else:
        p_real, p_imag = moved_probe(marks, probe, mine, other, power)
        new_probe[0] = p_real
        new_probe[1] = p_imag
    mean = jnp.sum(p_real * p_real + p_imag * p_imag) / (size * size)
    scale = object_step / (mean + tiny_value)

    even, even_t, odd, odd_t = (
        (tables[2 * n], tables[2 * n + 1]) for n in range(4)
    )
    pg_real = jnp.zeros((size, size), jnp.float32)
    pg_imag = jnp.zeros((size, size), jnp.float32)
    power_sum = jnp.zeros((), jnp.float32)
    for slot in range(slots):
        row = jnp.clip(marks[2 + 2 * slot], 0, HALO)
        col = jnp.clip(marks[3 + 2 * slot], 0, HALO)
        live = slot < marks[0]
        z_real = take_window(ext, 0, row, col, size)
        z_imag = take_window(ext, 1, row, col, size)
        psi_real = p_real * z_real - p_imag * z_imag
        psi_imag = p_real * z_imag + p_imag * z_real
        plus = jnp.concatenate(
            [psi_real[:, :half] + psi_real[:, half:], psi_imag[:, :half] + psi_imag[:, half:]], axis=1
        )
        minus = jnp.concatenate(
            [psi_real[:, :half] - psi_real[:, half:], psi_imag[:, :half] - psi_imag[:, half:]], axis=1
        )
        a_even = mul3(split(plus), even)
        a_odd = mul3(split(minus), odd)
        y_real = jnp.concatenate([a_even[:, :half], a_odd[:, :half]], axis=1)
        y_imag = jnp.concatenate([a_even[:, half:], a_odd[:, half:]], axis=1)
        plus = jnp.concatenate([y_real[:half] + y_real[half:], y_imag[:half] + y_imag[half:]], axis=0)
        minus = jnp.concatenate([y_real[:half] - y_real[half:], y_imag[:half] - y_imag[half:]], axis=0)
        sums = []
        for part, (data, table, back) in enumerate(((plus, even_t, even), (minus, odd_t, odd))):
            hat = mul3(table, split(data))
            h_real = hat[:half]
            h_imag = hat[half:]
            magnitude = h_real * h_real + h_imag * h_imag
            measured = amp[slot, part * half : (part + 1) * half, :]
            ratio = measured * lax.rsqrt(magnitude + smooth_floor) - 1.0
            scaled = jnp.concatenate([h_real * ratio, h_imag * ratio], axis=0)
            sums.append(mul3(back, split(scaled)))
        top = sums[0] + sums[1]
        bottom = sums[0] - sums[1]
        z_even = jnp.concatenate(
            [
                jnp.concatenate([top[:half, :half], top[half:, :half]], axis=1),
                jnp.concatenate([bottom[:half, :half], bottom[half:, :half]], axis=1),
            ],
            axis=0,
        )
        z_odd = jnp.concatenate(
            [
                jnp.concatenate([top[:half, half:], top[half:, half:]], axis=1),
                jnp.concatenate([bottom[:half, half:], bottom[half:, half:]], axis=1),
            ],
            axis=0,
        )
        u = mul3(split(z_even), even_t)
        v = mul3(split(z_odd), odd_t)
        plus = u + v
        minus = u - v
        d_real = jnp.concatenate([plus[:, :half], minus[:, :half]], axis=1)
        d_imag = jnp.concatenate([plus[:, half:], minus[:, half:]], axis=1)
        d_real = jnp.where(live, d_real, 0.0)
        d_imag = jnp.where(live, d_imag, 0.0)
        pg_real = pg_real + (z_real * d_real + z_imag * d_imag)
        pg_imag = pg_imag + (z_real * d_imag - z_imag * d_real)
        terms[slot, 0] = (p_real * d_real + p_imag * d_imag) * scale
        terms[slot, 1] = (p_real * d_imag - p_imag * d_real) * scale
        window_power = jnp.sum(z_real * z_real + z_imag * z_imag)
        power_sum = power_sum + jnp.where(live, window_power, 0.0)

    second = marks[1] == 1
    per = 2 * size // members
    for half_at in range(2):
        columns = slice(half_at * half, (half_at + 1) * half)
        kept = jnp.where(second, pg_imag[:, columns], pg_real[:, columns])
        given = jnp.where(second, pg_real[:, columns], pg_imag[:, columns])
        for m in range(members // 2):
            at = (half_at * members // 2 + m) * (per + 2)
            for ref, value in ((keep, kept), (give, given)):
                ref[at : at + per, :] = value[m * per : (m + 1) * per, :]
                ref[at + per : at + per + 2, :] = jnp.full((2, half), power_sum)


def moved_probe(marks, probe, mine, other, power):
    size = probe.shape[1]
    second = marks[1] == 1
    factor = 1.0 / (power[0:1, 0:1] / (size * size) + tiny_value)
    p_real = probe[0]
    p_imag = probe[1]
    one = jnp.concatenate([mine[:size, :], mine[size:, :]], axis=1)
    two = jnp.concatenate([other[:size, :], other[size:, :]], axis=1)
    m_real = p_real + jnp.where(second, two, one) * factor
    m_imag = p_imag + jnp.where(second, one, two) * factor
    old = jnp.sum(p_real * p_real + p_imag * p_imag)
    new = jnp.sum(m_real * m_real + m_imag * m_imag)
    gain = jnp.sqrt(jnp.full((1, 1), old) / (jnp.full((1, 1), new) + tiny_value))
    return m_real * gain, m_imag * gain


def probe_kernel(marks, probe, mine, other, power, out):
    real, imag = moved_probe(marks, probe, mine, other, power)
    out[0] = real
    out[1] = imag


def place_kernel(marks, tile, terms, partial, rim_right, rim_low, *rest):
    ext = rest[-1]
    size = tile.shape[1]
    slots = terms.shape[0]
    ext[...] = jnp.zeros_like(ext)
    for slot in range(slots):
        row = jnp.clip(marks[2 + 2 * slot], 0, HALO)
        col = jnp.clip(marks[3 + 2 * slot], 0, HALO)
        for part in range(2):
            add_window(ext, part, row, col, terms[slot, part])
    partial[...] = tile[...] + ext[:, :size, :size]
    rim_right[...] = ext[:, : rim_right.shape[1], size:]
    rim_low[...] = ext[:, size : size + HALO, :size]
    if len(rest) > 1:
        rest[0][...] = ext[:, size : size + HALO, size:]


def update_kernel(partial, from_left, from_above, from_corner, out, below):
    out[...] = partial[...]
    out[:, :, :HALO] += from_left[...]
    out[:, :HALO, :] += from_above[...]
    out[:, :HALO, :HALO] += from_corner[...]
    below[...] = out[:, :HALO, :]


def merge_kernel(rim_low, from_left, out):
    size = rim_low.shape[2]
    out[...] = rim_low[...]
    out[:, :, :HALO] += from_left[:, size:, :]


def finish_kernel(partial, from_left, from_above, out):
    size = partial.shape[1]
    out[...] = partial[...]
    out[:, :, :HALO] += from_left[:, :size, :]
    out[:, :HALO, :] += from_above[...]


def join_kernel(tile, low, out):
    size = tile.shape[1]
    out[:, :size, :] = tile[:, :, :HALO]
    out[:, size:, :] = low[:, :, :HALO]


def fold_kernel(members, copies, keep, source, out, *power):
    count = source.shape[0]
    n = count // members
    step = 4 * n
    groups = count // step
    total = source[0:step, :]
    for g in range(1, groups):
        total = total + source[g * step : (g + 1) * step, :]
    summed = total[0:n] + total[n : 2 * n] + (total[2 * n : 3 * n] + total[3 * n :])
    for c in range(copies):
        out[c * keep : (c + 1) * keep, :] = summed[:keep]
    if power:
        power[0][...] = jnp.broadcast_to(summed[n - 1 : n], power[0].shape)


def call(kernel, outs, specs, *args, scratch=(), grant=2):
    return pl.pallas_call(
        kernel,
        out_shape=[jax.ShapeDtypeStruct(shape, jnp.float32) for shape in outs],
        in_specs=specs,
        out_specs=[VMEM] * len(outs),
        scratch_shapes=[pltpu.VMEM(shape, jnp.float32) for shape in scratch],
        compiler_params=pltpu.CompilerParams(vmem_limit_bytes=grant << 20),
    )(*args)


def shards(object_field, probe_field, amplitudes, offsets, counts):
    _, size, _ = object_field.shape
    half = size // 2
    slots = amplitudes.shape[0]
    margin = HALO
    edge_shapes = [(2, margin, size), (2, size, margin), (2, margin, margin)]
    wide_groups, line_groups = device_groups(lax.axis_size("row"), lax.axis_size("col"))
    wide, line = len(wide_groups[0]), len(line_groups[0])
    per = 2 * size // wide
    held = wide * (per + 2)
    tables = jnp.asarray(make_tables(size))
    order = np.concatenate([np.arange(0, size, 2), np.arange(1, size, 2)])
    pick = jnp.asarray(np.eye(size)[:, order].astype(jnp.bfloat16))
    core = jnp.bitwise_and(lax.axis_index("col"), 1).astype(jnp.int32)
    marks = jnp.concatenate([counts.reshape(1), core.reshape(1), offsets.reshape(2 * slots)])

    current = object_field
    edges = call(edges_kernel, edge_shapes, [VMEM], current)
    amp, probe_now = call(
        order_kernel,
        [amplitudes.shape, probe_field.shape],
        [VMEM] * 3,
        amplitudes,
        pick,
        probe_field,
        scratch=[(2 * slots, size, half)],
    )
    low = shifted(edges[0], -1, 0)
    right = shifted(edges[1], 0, -1)
    corner = shifted(edges[2], -1, -1)
    mine = other = power = None
    for outer_step in range(OUTER):
        first = outer_step == 0
        outs = [(held, half), (held, half), (slots, 2, size, size)]
        args = [marks, current, low, right] + ([corner] if first else []) + [probe_now]
        if not first:
            outs.append((2, size, size))
            args += [mine, other, power]
        args += [amp, tables]
        done = call(
            functools.partial(solve_kernel, first, wide),
            outs,
            [SMEM] + [VMEM] * (len(args) - 1),
            *args,
            scratch=[(2, size + margin + SUB, size + margin)],
            grant=8,
        )
        keep, give, terms = done[:3]
        if not first:
            probe_now = done[3]
        given = swap_cores(give)
        last = outer_step == OUTER - 1
        if last:
            rim_shapes = [(2, size + margin, margin), edge_shapes[0]]
        else:
            rim_shapes = [edge_shapes[1], edge_shapes[0], edge_shapes[2]]
        partial, rim_right, rim_low, *rim_corner = call(
            place_kernel,
            [current.shape] + rim_shapes,
            [SMEM, VMEM, VMEM],
            marks,
            current,
            terms,
            scratch=[(2, size + margin + SUB, size + margin)],
            grant=3,
        )
        from_left = shifted(rim_right, 0, 1)
        if not last:
            from_above = shifted(rim_low, 1, 0)
            from_corner = shifted(rim_corner[0], 1, 1)
        if last:
            (merged,) = call(
                merge_kernel, [edge_shapes[0]], [VMEM] * 2, rim_low, from_left
            )
            from_above = shifted(merged, 1, 0)
        arrived = exchange(keep + given, wide_groups)
        (copies,) = call(
            functools.partial(fold_kernel, wide, line, per + 2),
            [(line * (per + 2), half)],
            [VMEM],
            arrived,
        )
        arrived = exchange(copies, line_groups)
        copies, power = call(
            functools.partial(fold_kernel, line, wide, per),
            [(wide * per, half), (8, half)],
            [VMEM],
            arrived,
        )
        mine = exchange(copies, wide_groups)
        other = swap_cores(mine)
        if last:
            (current,) = call(
                finish_kernel,
                [current.shape],
                [VMEM] * 3,
                partial,
                from_left,
                from_above,
            )
        else:
            current, below = call(
                update_kernel,
                [current.shape, edge_shapes[0]],
                [VMEM] * 4,
                partial,
                from_left,
                from_above,
                from_corner,
            )
            low = shifted(below, -1, 0)
            (joined,) = call(
                join_kernel, [(2, size + margin, margin)], [VMEM] * 2, current, low
            )
            right = shifted(joined, 0, -1)
    (probe_now,) = call(
        probe_kernel,
        [probe_field.shape],
        [SMEM] + [VMEM] * 4,
        marks,
        probe_now,
        mine,
        other,
        power,
    )
    return (current, probe_now)


def solution(mesh):
    return jax.shard_map(
        shards,
        mesh=mesh,
        in_specs=(
            P(None, "row", "col"),
            P(),
            P("row", "col", None),
            P("row", "col", None, None),
            P("row", "col"),
        ),
        out_specs=(P(None, "row", "col"), P()),
        check_vma=False,
    )
```

```python
import functools

import jax
import jax.numpy as jnp
import numpy as np
from jax import lax
from jax.experimental import pallas as pl
from jax.experimental.pallas import tpu as pltpu
from jax.sharding import PartitionSpec as P


HALO = 128
SUB, LANE = 8, 128
OUTER = 2
NEAR = 8

smooth_floor = 0.5
object_step = 0.5
tiny_value = 1e-06

VMEM = pl.BlockSpec(memory_space=pltpu.VMEM)
SMEM = pl.BlockSpec(memory_space=pltpu.SMEM)


def shifted(value, down_by, across_by):
    down = lax.axis_size("row")
    across = lax.axis_size("col")
    pairs = [
        (r * across + c, (r + down_by) * across + c + across_by)
        for r in range(down)
        for c in range(across)
        if 0 <= r + down_by < down and 0 <= c + across_by < across
    ]
    return lax.ppermute(value, ("row", "col"), pairs)


def device_groups(down, across):
    far = down // NEAR
    wide_groups = [
        [(y * NEAR + z) * across + x * 2 + core for y in range(far) for x in range(across // 2)]
        for z in range(NEAR)
        for core in range(2)
    ]
    line_groups = [
        [(y * NEAR + z) * across + c for z in range(NEAR)]
        for y in range(far)
        for c in range(across)
    ]
    return wide_groups, line_groups


def swap_cores(value):
    across = lax.axis_size("col")
    return lax.ppermute(value, "col", [(c, c ^ 1) for c in range(across)])


def exchange(rows, groups):
    count, lanes = rows.shape
    paired = rows.reshape(count // 2, 2, lanes)
    moved = lax.all_to_all(
        paired, ("row", "col"), 0, 0, tiled=True, axis_index_groups=groups
    )
    return moved.reshape(count, lanes)


def make_tables(length):
    half = length // 2
    out = []
    for start in (0, 1):
        first = np.arange(half)[:, None]
        second = np.arange(start, length, 2)[None, :]
        angle = -2.0 * np.pi * ((first * second) % length) / length
        real = np.cos(angle) / np.sqrt(length)
        imag = np.sin(angle) / np.sqrt(length)
        block = np.block([[real, imag], [-imag, real]])
        for table in (block, block.T):
            high = table.astype(np.float32).astype(jnp.bfloat16)
            low = (table - high.astype(np.float64)).astype(np.float32)
            out += [high, low.astype(jnp.bfloat16)]
    return np.stack(out)


def split(value):
    high = value.astype(jnp.bfloat16)
    low = (value - high.astype(jnp.float32)).astype(jnp.bfloat16)
    return high, low


def mul(left, right):
    return jnp.dot(left, right, preferred_element_type=jnp.float32)


def right_mul(data, tables, at):
    high, low = split(data)
    rows = data.shape[0]
    both = mul(jnp.concatenate([high, low], axis=0), tables[at * 2])
    return both[:rows] + (both[rows:] + mul(high, tables[at * 2 + 1]))


def left_mul(tables, at, data):
    high, low = split(data)
    rows = data.shape[0]
    table = tables[at * 2 : at * 2 + 2].reshape(2 * rows, rows)
    both = mul(table, high)
    return both[:rows] + (both[rows:] + mul(tables[at * 2], low))


def edges_kernel(tile, low, right, corner):
    low[...] = tile[:, :HALO, :]
    right[...] = tile[:, :, :HALO]
    corner[...] = tile[:, :HALO, :HALO]


def order_kernel(amplitudes, pick, probe, out, probe_out, held):
    slots, size, _ = amplitudes.shape
    half = size // 2
    probe_out[...] = probe[...]
    for slot in range(slots):
        rest = amplitudes[slot]
        total = jnp.zeros((size, size), jnp.float32)
        for _ in range(3):
            piece = rest.astype(jnp.bfloat16)
            total = total + mul(piece, pick[...])
            rest = rest - piece.astype(jnp.float32)
        for side in range(2):
            held[2 * slot + side] = total[:, side * half : (side + 1) * half]
            for part in range(2):
                out[slot, part * half : (part + 1) * half, side * half : (side + 1) * half] = held[
                    2 * slot + side, pl.ds(part, half, 2), :
                ]


def halves(row):
    rest = jnp.bitwise_and(row, SUB - 1)
    base = pl.multiple_of(row - rest, SUB)
    at_row = lax.broadcasted_iota(jnp.int32, (1, SUB, LANE), 1)
    at_col = lax.broadcasted_iota(jnp.int32, (1, SUB, LANE), 2)
    return rest, base, at_row, at_col


def take_window(ext, part, row, col, size):
    rest, base, at_row, at_col = halves(row)
    wide = ext[part, pl.ds(base, size + SUB), :]
    wide = wide.reshape(size // SUB + 1, SUB, wide.shape[1])
    turn_col = jnp.bitwise_and(LANE - col, LANE - 1)
    turn_row = jnp.bitwise_and(SUB - rest, SUB - 1)
    turned = []
    for t in range(wide.shape[2] // LANE):
        block = pltpu.roll(wide[:, :, t * LANE : (t + 1) * LANE], turn_col, 2)
        turned.append(pltpu.roll(block, turn_row, 1))
    out = []
    for t in range(len(turned) - 1):
        block = jnp.where(at_col < LANE - col, turned[t], turned[t + 1])
        block = jnp.where(at_row < SUB - rest, block[:-1], block[1:])
        out.append(block.reshape(size, LANE))
    return jnp.concatenate(out, axis=1)


def add_window(ext, part, row, col, value):
    size = value.shape[0]
    rest, base, at_row, at_col = halves(row)
    turn_col = jnp.bitwise_and(col, LANE - 1)
    blocks = []
    for t in range(size // LANE):
        block = value[:, t * LANE : (t + 1) * LANE].reshape(size // SUB, SUB, LANE)
        block = pltpu.roll(pltpu.roll(block, turn_col, 2), rest, 1)
        edge = jnp.zeros((1, SUB, LANE), jnp.float32)
        blocks.append(
            jnp.where(
                at_row < rest,
                jnp.concatenate([edge, block], axis=0),
                jnp.concatenate([block, edge], axis=0),
            )
        )
    none = jnp.zeros_like(blocks[0])
    blocks = [none] + blocks + [none]
    for t in range(len(blocks) - 1):
        placed = jnp.where(at_col < col, blocks[t], blocks[t + 1])
        at = (part, pl.ds(base, size + SUB), slice(t * LANE, (t + 1) * LANE))
        ext[at] = ext[at] + placed.reshape(size + SUB, LANE)


def solve_kernel(first, members, *refs):
    if first:
        (marks, tile, low, right, corner, probe, amp, tables) = refs[:8]
        keep, give, terms, ext = refs[8:]
    else:
        (marks, tile, low, right, probe, mine, other, power, amp, tables) = refs[:10]
        keep, give, terms, new_probe, ext = refs[10:]
    size = tile.shape[1]
    half = size // 2
    slots = amp.shape[0]
    ext[:, :size, :size] = tile[...]
    ext[:, size : size + HALO, :size] = low[...]
    if first:
        ext[:, :size, size:] = right[...]
        ext[:, size : size + HALO, size:] = corner[...]
    else:
        ext[:, : size + HALO, size:] = right[...]
    ext[:, size + HALO :, :] = jnp.zeros((2, SUB, size + HALO), jnp.float32)

    if first:
        p_real = probe[0]
        p_imag = probe[1]
    else:
        p_real, p_imag = moved_probe(marks, probe, mine, other, power)
        new_probe[0] = p_real
        new_probe[1] = p_imag
    mean = jnp.sum(p_real * p_real + p_imag * p_imag) / (size * size)
    scale = object_step / (mean + tiny_value)

    even, even_t, odd, odd_t = range(4)
    z_real, z_imag, psi = [], [], []
    power_sum = jnp.zeros((), jnp.float32)
    for slot in range(slots):
        row = jnp.clip(marks[2 + 2 * slot], 0, HALO)
        col = jnp.clip(marks[3 + 2 * slot], 0, HALO)
        z_r = take_window(ext, 0, row, col, size)
        z_i = take_window(ext, 1, row, col, size)
        window_power = jnp.sum(z_r * z_r + z_i * z_i)
        power_sum = power_sum + jnp.where(slot < marks[0], window_power, 0.0)
        psi.append((p_real * z_r - p_imag * z_i, p_real * z_i + p_imag * z_r))
        z_real.append(z_r)
        z_imag.append(z_i)

    def both(make):
        return jnp.concatenate([make(*psi[slot]) for slot in range(slots)], axis=0)

    a_even = right_mul(
        both(lambda r, i: jnp.concatenate([r[:, :half] + r[:, half:], i[:, :half] + i[:, half:]], axis=1)),
        tables,
        even,
    )
    a_odd = right_mul(
        both(lambda r, i: jnp.concatenate([r[:, :half] - r[:, half:], i[:, :half] - i[:, half:]], axis=1)),
        tables,
        odd,
    )
    plus, minus = [], []
    for slot in range(slots):
        top = slice(slot * size, slot * size + half)
        bottom = slice(slot * size + half, (slot + 1) * size)
        up = jnp.concatenate([a_even[top], a_odd[top]], axis=1)
        down = jnp.concatenate([a_even[bottom], a_odd[bottom]], axis=1)
        total, rest = up + down, up - down
        for out, value in ((plus, total), (minus, rest)):
            real = jnp.concatenate([value[:, :half], value[:, size : size + half]], axis=1)
            imag = jnp.concatenate([value[:, half:size], value[:, size + half :]], axis=1)
            out.append(jnp.concatenate([real, imag], axis=0))
    sums = []
    for part, (data, table, back) in enumerate(((plus, even_t, even), (minus, odd_t, odd))):
        hat = left_mul(tables, table, jnp.concatenate(data, axis=1))
        h_real = hat[:half]
        h_imag = hat[half:]
        magnitude = h_real * h_real + h_imag * h_imag
        measured = jnp.concatenate(
            [amp[slot, part * half : (part + 1) * half, :] for slot in range(slots)], axis=1
        )
        ratio = measured * lax.rsqrt(magnitude + smooth_floor) - 1.0
        scaled = jnp.concatenate([h_real * ratio, h_imag * ratio], axis=0)
        sums.append(left_mul(tables, back, scaled))
    top = sums[0] + sums[1]
    bottom = sums[0] - sums[1]
    stacked = []
    for side in range(2):
        rows = []
        for slot in range(slots):
            columns = slice(slot * size + side * half, slot * size + (side + 1) * half)
            for value in (top, bottom):
                rows.append(jnp.concatenate([value[:half, columns], value[half:, columns]], axis=1))
        stacked.append(jnp.concatenate(rows, axis=0))
    u = right_mul(stacked[0], tables, even_t)
    v = right_mul(stacked[1], tables, odd_t)
    plus = u + v
    minus = u - v
    pg_real = jnp.zeros((size, size), jnp.float32)
    pg_imag = jnp.zeros((size, size), jnp.float32)
    for slot in range(slots):
        live = slot < marks[0]
        rows = slice(slot * size, (slot + 1) * size)
        d_real = jnp.concatenate([plus[rows, :half], minus[rows, :half]], axis=1)
        d_imag = jnp.concatenate([plus[rows, half:], minus[rows, half:]], axis=1)
        d_real = jnp.where(live, d_real, 0.0)
        d_imag = jnp.where(live, d_imag, 0.0)
        pg_real = pg_real + (z_real[slot] * d_real + z_imag[slot] * d_imag)
        pg_imag = pg_imag + (z_real[slot] * d_imag - z_imag[slot] * d_real)
        terms[slot, 0] = (p_real * d_real + p_imag * d_imag) * scale
        terms[slot, 1] = (p_real * d_imag - p_imag * d_real) * scale

    second = marks[1] == 1
    per = 2 * size // members
    for half_at in range(2):
        columns = slice(half_at * half, (half_at + 1) * half)
        kept = jnp.where(second, pg_imag[:, columns], pg_real[:, columns])
        given = jnp.where(second, pg_real[:, columns], pg_imag[:, columns])
        for m in range(members // 2):
            at = (half_at * members // 2 + m) * (per + 2)
            for ref, value in ((keep, kept), (give, given)):
                ref[at : at + per, :] = value[m * per : (m + 1) * per, :]
                ref[at + per : at + per + 2, :] = jnp.full((2, half), power_sum)


def moved_probe(marks, probe, mine, other, power):
    size = probe.shape[1]
    second = marks[1] == 1
    factor = 1.0 / (power[0:1, 0:1] / (size * size) + tiny_value)
    p_real = probe[0]
    p_imag = probe[1]
    one = jnp.concatenate([mine[:size, :], mine[size:, :]], axis=1)
    two = jnp.concatenate([other[:size, :], other[size:, :]], axis=1)
    m_real = p_real + jnp.where(second, two, one) * factor
    m_imag = p_imag + jnp.where(second, one, two) * factor
    old = jnp.sum(p_real * p_real + p_imag * p_imag)
    new = jnp.sum(m_real * m_real + m_imag * m_imag)
    gain = jnp.sqrt(jnp.full((1, 1), old) / (jnp.full((1, 1), new) + tiny_value))
    return m_real * gain, m_imag * gain


def probe_kernel(marks, probe, mine, other, power, out):
    real, imag = moved_probe(marks, probe, mine, other, power)
    out[0] = real
    out[1] = imag


def place_kernel(marks, tile, terms, partial, rim_right, rim_low, *rest):
    ext = rest[-1]
    size = tile.shape[1]
    slots = terms.shape[0]
    ext[...] = jnp.zeros_like(ext)
    for slot in range(slots):
        row = jnp.clip(marks[2 + 2 * slot], 0, HALO)
        col = jnp.clip(marks[3 + 2 * slot], 0, HALO)
        for part in range(2):
            add_window(ext, part, row, col, terms[slot, part])
    partial[...] = tile[...] + ext[:, :size, :size]
    rim_right[...] = ext[:, : rim_right.shape[1], size:]
    rim_low[...] = ext[:, size : size + HALO, :size]
    if len(rest) > 1:
        rest[0][...] = ext[:, size : size + HALO, size:]


def update_kernel(partial, from_left, from_above, from_corner, out, below):
    out[...] = partial[...]
    out[:, :, :HALO] += from_left[...]
    out[:, :HALO, :] += from_above[...]
    out[:, :HALO, :HALO] += from_corner[...]
    below[...] = out[:, :HALO, :]


def merge_kernel(rim_low, from_left, out):
    size = rim_low.shape[2]
    out[...] = rim_low[...]
    out[:, :, :HALO] += from_left[:, size:, :]


def finish_kernel(partial, from_left, from_above, out):
    size = partial.shape[1]
    out[...] = partial[...]
    out[:, :, :HALO] += from_left[:, :size, :]
    out[:, :HALO, :] += from_above[...]


def join_kernel(tile, low, out):
    size = tile.shape[1]
    out[:, :size, :] = tile[:, :, :HALO]
    out[:, size:, :] = low[:, :, :HALO]


def fold_kernel(members, copies, keep, source, out, *power):
    count = source.shape[0]
    n = count // members
    step = 4 * n
    groups = count // step
    total = source[0:step, :]
    for g in range(1, groups):
        total = total + source[g * step : (g + 1) * step, :]
    summed = total[0:n] + total[n : 2 * n] + (total[2 * n : 3 * n] + total[3 * n :])
    for c in range(copies):
        out[c * keep : (c + 1) * keep, :] = summed[:keep]
    if power:
        power[0][...] = jnp.broadcast_to(summed[n - 1 : n], power[0].shape)


def call(kernel, outs, specs, *args, scratch=(), grant=2):
    return pl.pallas_call(
        kernel,
        out_shape=[jax.ShapeDtypeStruct(shape, jnp.float32) for shape in outs],
        in_specs=specs,
        out_specs=[VMEM] * len(outs),
        scratch_shapes=[pltpu.VMEM(shape, jnp.float32) for shape in scratch],
        compiler_params=pltpu.CompilerParams(vmem_limit_bytes=grant << 20),
    )(*args)


def shards(object_field, probe_field, amplitudes, offsets, counts):
    _, size, _ = object_field.shape
    half = size // 2
    slots = amplitudes.shape[0]
    margin = HALO
    edge_shapes = [(2, margin, size), (2, size, margin), (2, margin, margin)]
    wide_groups, line_groups = device_groups(lax.axis_size("row"), lax.axis_size("col"))
    wide, line = len(wide_groups[0]), len(line_groups[0])
    per = 2 * size // wide
    held = wide * (per + 2)
    tables = jnp.asarray(make_tables(size))
    order = np.concatenate([np.arange(0, size, 2), np.arange(1, size, 2)])
    pick = jnp.asarray(np.eye(size)[:, order].astype(jnp.bfloat16))
    core = jnp.bitwise_and(lax.axis_index("col"), 1).astype(jnp.int32)
    marks = jnp.concatenate([counts.reshape(1), core.reshape(1), offsets.reshape(2 * slots)])

    current = object_field
    edges = call(edges_kernel, edge_shapes, [VMEM], current)
    amp, probe_now = call(
        order_kernel,
        [amplitudes.shape, probe_field.shape],
        [VMEM] * 3,
        amplitudes,
        pick,
        probe_field,
        scratch=[(2 * slots, size, half)],
    )
    low = shifted(edges[0], -1, 0)
    right = shifted(edges[1], 0, -1)
    corner = shifted(edges[2], -1, -1)
    mine = other = power = None
    for outer_step in range(OUTER):
        first = outer_step == 0
        outs = [(held, half), (held, half), (slots, 2, size, size)]
        args = [marks, current, low, right] + ([corner] if first else []) + [probe_now]
        if not first:
            outs.append((2, size, size))
            args += [mine, other, power]
        args += [amp, tables]
        done = call(
            functools.partial(solve_kernel, first, wide),
            outs,
            [SMEM] + [VMEM] * (len(args) - 1),
            *args,
            scratch=[(2, size + margin + SUB, size + margin)],
            grant=8,
        )
        keep, give, terms = done[:3]
        if not first:
            probe_now = done[3]
        given = swap_cores(give)
        last = outer_step == OUTER - 1
        if last:
            rim_shapes = [(2, size + margin, margin), edge_shapes[0]]
        else:
            rim_shapes = [edge_shapes[1], edge_shapes[0], edge_shapes[2]]
        partial, rim_right, rim_low, *rim_corner = call(
            place_kernel,
            [current.shape] + rim_shapes,
            [SMEM, VMEM, VMEM],
            marks,
            current,
            terms,
            scratch=[(2, size + margin + SUB, size + margin)],
            grant=3,
        )
        if not last:
            from_corner = shifted(rim_corner[0], 1, 1)
            from_above = shifted(rim_low, 1, 0)
        from_left = shifted(rim_right, 0, 1)
        if last:
            (merged,) = call(
                merge_kernel, [edge_shapes[0]], [VMEM] * 2, rim_low, from_left
            )
            from_above = shifted(merged, 1, 0)
        arrived = exchange(keep + given, wide_groups)
        (copies,) = call(
            functools.partial(fold_kernel, wide, line, per + 2),
            [(line * (per + 2), half)],
            [VMEM],
            arrived,
        )
        arrived = exchange(copies, line_groups)
        copies, power = call(
            functools.partial(fold_kernel, line, wide, per),
            [(wide * per, half), (8, half)],
            [VMEM],
            arrived,
        )
        mine = exchange(copies, wide_groups)
        other = swap_cores(mine)
        if last:
            (current,) = call(
                finish_kernel,
                [current.shape],
                [VMEM] * 3,
                partial,
                from_left,
                from_above,
            )
        else:
            current, below = call(
                update_kernel,
                [current.shape, edge_shapes[0]],
                [VMEM] * 4,
                partial,
                from_left,
                from_above,
                from_corner,
            )
            low = shifted(below, -1, 0)
            (joined,) = call(join_kernel, [(2, size + margin, margin)], [VMEM] * 2, current, low)
            right = shifted(joined, 0, -1)
    (probe_now,) = call(
        probe_kernel,
        [probe_field.shape],
        [SMEM] + [VMEM] * 4,
        marks,
        probe_now,
        mine,
        other,
        power,
    )
    return (current, probe_now)


def solution(mesh):
    return jax.shard_map(
        shards,
        mesh=mesh,
        in_specs=(
            P(None, "row", "col"),
            P(),
            P("row", "col", None),
            P("row", "col", None, None),
            P("row", "col"),
        ),
        out_specs=(P(None, "row", "col"), P()),
        check_vma=False,
    )
```
